32 devices in a mesh: dp: 8 (over y, x, core), tensor: 4 (over z).
Axes of the slice: x: 2, y: 2, z: 4, core: 2. Of those that a mesh axis runs over, the one named last changes fastest.
Arguments:
- tokens: bfloat16 [3072, 8192], P('dp', 'tensor'), may hold values from -6 to 6
- up_first: bfloat16 [16, 512, 512], P('tensor'), may hold values from -0.25 to 0.25
- up_second: bfloat16 [16, 512, 2048], P('tensor'), may hold values from -0.25 to 0.25
- down_first: bfloat16 [16, 2048, 512], P('tensor'), may hold values from -0.125 to 0.125
- down_second: bfloat16 [16, 512, 512], P('tensor'), may hold values from -0.25 to 0.25
- cotangent: bfloat16 [3072, 8192], P('dp', 'tensor'), may hold values from -6 to 6
Outputs:
- layer_out: bfloat16 [3072, 8192], P('dp', 'tensor')
- grad_tokens: bfloat16 [3072, 8192], P('dp', 'tensor')
- grad_up_first: float32 [16, 512, 512], P('tensor', 'dp')
- grad_up_second: float32 [16, 512, 2048], P('tensor', 'dp')
- grad_down_first: float32 [16, 2048, 512], P('tensor', 'dp')
- grad_down_second: float32 [16, 512, 512], P('tensor', 'dp')
The draws below stay inside these ranges and needn't reach their ends.
All inputs are finite; a program needn't handle non-finite values.
Results may differ from the reference program's by a relative error of at most 0.023.
Values may be sent and summed in bfloat16 or wider, within the bound.
No kernel may reach another device: no remote copies, remote signals or barrier semaphores. Data moves between devices by JAX's collectives and lax.ppermute only.
A program may use at most 128 MiB of HBM per device.

```python
import jax
import jax.numpy as jnp
from jax import lax

D = 8192
H = 32768
NB = 16
TOK_DEV = 384
BS = 512
HB = 2048
TOKENS = 3072
N_DP = 8


def shard_levels(key, dims, shards, low, largest):
    gain, own = 1.0, jax.random.fold_in(key, 6)
    for dim, parts in shards:
        heights = jnp.exp(jax.random.uniform(jax.random.fold_in(own, dim), (parts,), jnp.float32, low / len(shards), largest / len(shards)))
        gain = gain * jnp.repeat(heights, dims[dim] // parts).reshape([-1 if axis == dim else 1 for axis in range(len(dims))])
    return gain


def gaussian(stream_key, dims, spread, bound, split=(), held_as=jnp.bfloat16):
    factor_of = shard_levels(stream_key, dims, split, -0.22, 0.18) if split else 1.0
    drawn = jax.random.normal(stream_key, dims, jnp.float32) * spread * factor_of
    return jnp.minimum(jnp.maximum(drawn, -bound), bound).astype(held_as)


def setup_inputs(seed: int = 0) -> dict:
    seeds = jax.random.split(jax.random.key(seed), 7)
    return {
        "tokens": gaussian(seeds[0], (TOKENS, D), 1.0, 6.0, ((0, 8), (1, 4))),
        "up_first": gaussian(seeds[1], (NB, BS, BS), BS ** -0.5, 0.25, ((0, 4),)),
        "up_second": gaussian(seeds[2], (NB, BS, HB), BS ** -0.5, 0.25, ((0, 4),)),
        "down_first": gaussian(seeds[3], (NB, HB, BS), HB ** -0.5, 0.125, ((0, 4),)),
        "down_second": gaussian(seeds[4], (NB, BS, BS), BS ** -0.5, 0.25, ((0, 4),)),
        "cotangent": gaussian(seeds[5], (TOKENS, D), 1.0, 6.0, ((0, 8), (1, 4))),
    }


gelu_coeff = 0.7978845608028654
cubic_coeff = 0.044715


def gelu_pair(hidden):
    inner_arg = gelu_coeff * (hidden + cubic_coeff * hidden * hidden * hidden)
    tangent = jnp.tanh(inner_arg)
    gelu_value = 0.5 * hidden * (1.0 + tangent)
    gelu_slope = 0.5 * (1.0 + tangent) + 0.5 * hidden * (1.0 - tangent * tangent) * gelu_coeff * (1.0 + 3.0 * cubic_coeff * hidden * hidden)
    return gelu_value, gelu_slope


def regroup_rows(values, row_count):
    slice_width = D // (NB * NB)
    return values.reshape(row_count, NB, NB, slice_width).transpose(0, 2, 1, 3).reshape(row_count, NB, NB * slice_width)


def reference(tokens, up_first, up_second, down_first, down_second, cotangent):
    block_size = D // NB
    grad_scale = TOKENS ** -0.5
    first_wide = up_first.astype(jnp.float32)
    second_wide = up_second.astype(jnp.float32)
    third_wide = down_first.astype(jnp.float32)
    fourth_wide = down_second.astype(jnp.float32)
    token_groups = tokens.reshape(N_DP, TOK_DEV, D)
    grad_groups = cotangent.reshape(N_DP, TOK_DEV, D)

    def rounded(term_value):
        narrow = lax.optimization_barrier((grad_scale * term_value).astype(jnp.bfloat16))
        return narrow.astype(jnp.float32)

    def shard_step(totals, inputs_pair):
        x_part, g_part = inputs_pair
        x_three = x_part.astype(jnp.float32).reshape(TOK_DEV, NB, block_size)
        mixed_up = jnp.einsum("tbi,bio->tbo", x_three, first_wide).astype(jnp.bfloat16)
        regrouped_up = regroup_rows(mixed_up, TOK_DEV).astype(jnp.float32)
        pre_act = jnp.einsum("tjm,jmo->tjo", regrouped_up, second_wide)
        gelu_value, gelu_slope = gelu_pair(pre_act)
        activated = gelu_value.astype(jnp.bfloat16).astype(jnp.float32)
        mixed_down = jnp.einsum("tjm,jmo->tjo", activated, third_wide).astype(jnp.bfloat16)
        regrouped_down = regroup_rows(mixed_down, TOK_DEV).astype(jnp.float32)
        branch = jnp.einsum("tkm,kmo->tko", regrouped_down, fourth_wide)
        layer_out = (x_three + branch).astype(jnp.bfloat16).reshape(TOK_DEV, D)
        grad_three = g_part.astype(jnp.float32).reshape(TOK_DEV, NB, block_size)
        back_down = jnp.einsum("tko,kmo->tkm", grad_three, fourth_wide).astype(jnp.bfloat16)
        grad_mid = regroup_rows(back_down, TOK_DEV).astype(jnp.float32)
        grad_act = jnp.einsum("tjo,jmo->tjm", grad_mid, third_wide)
        grad_pre = (grad_act * gelu_slope).astype(jnp.bfloat16).astype(jnp.float32)
        back_up = jnp.einsum("tjo,jmo->tjm", grad_pre, second_wide).astype(jnp.bfloat16)
        grad_in = regroup_rows(back_up, TOK_DEV).astype(jnp.float32)
        grad_tokens = (grad_three + jnp.einsum("tbo,bio->tbi", grad_in, first_wide)).astype(jnp.bfloat16).reshape(TOK_DEV, D)
        new_terms = (
            rounded(jnp.einsum("tbi,tbo->bio", x_three, grad_in)),
            rounded(jnp.einsum("tjm,tjo->jmo", regrouped_up, grad_pre)),
            rounded(jnp.einsum("tjm,tjo->jmo", activated, grad_mid)),
            rounded(jnp.einsum("tkm,tko->kmo", regrouped_down, grad_three)),
        )
        updated = tuple(running + addend for running, addend in zip(totals, new_terms))
        return updated, (layer_out, grad_tokens)

    start_totals = (
        jnp.zeros((NB, block_size, block_size), jnp.float32),
        jnp.zeros((NB, block_size, H // NB), jnp.float32),
        jnp.zeros((NB, H // NB, block_size), jnp.float32),
        jnp.zeros((NB, block_size, block_size), jnp.float32),
    )
    totals, stacked = lax.scan(shard_step, start_totals, (token_groups, grad_groups))
    layer_out = stacked[0].reshape(TOKENS, D)
    grad_tokens = stacked[1].reshape(TOKENS, D)
    return (layer_out, grad_tokens, totals[0], totals[1], totals[2], totals[3])
```

```python
import functools

import jax
import jax.numpy as jnp
from jax import lax
from jax.experimental import pallas as pl
from jax.experimental.pallas import tpu as pltpu
from jax.sharding import PartitionSpec as P

NB = 16
N_CHUNK = 2

gelu_coeff = 0.7978845608028654
cubic_coeff = 0.044715

BF16 = jnp.bfloat16
F32 = jnp.float32


def gelu_pair(hidden):
    inner_arg = gelu_coeff * (hidden + cubic_coeff * hidden * hidden * hidden)
    tangent = jnp.tanh(inner_arg)
    gelu_value = 0.5 * hidden * (1.0 + tangent)
    gelu_slope = 0.5 * (1.0 + tangent) + 0.5 * hidden * (1.0 - tangent * tangent) * gelu_coeff * (
        1.0 + 3.0 * cubic_coeff * hidden * hidden
    )
    return gelu_value, gelu_slope


def dot(a, b, ca, cb):
    return lax.dot_general(a, b, (((ca,), (cb,)), ((), ())), preferred_element_type=F32)


def params():
    return pltpu.CompilerParams(vmem_limit_bytes=52 * 1024 * 1024)


def spec(block, index_map):
    return pl.BlockSpec(block, index_map)


def enter(where, tokens, up_first, cotangent, down_second, sizes):
    T, L, BS, NT, G, SW, Q, _ = sizes
    rows = BS // (2 * Q)

    def kernel(where_ref, x_ref, w_ref, g_ref, d_ref, xt_ref, *rest):
        outs, (up_scr, back_scr) = rest[:-2], rest[-2:]
        turned = x_ref[...].T
        xt_ref[0] = turned.reshape(Q, 2, rows, T)
        up_scr[...] = dot(w_ref[0], turned, 0, 0).astype(BF16).reshape(NT, L, SW, T)
        back_scr[...] = dot(d_ref[0], g_ref[...], 1, 1).astype(BF16).reshape(NT, L, SW, T)
        for shift in range(NT):
            target = lax.rem(where_ref[0] + shift, NT)
            for chunk in range(N_CHUNK):
                out = outs[chunk * NT + shift]
                out[0, :, 0] = up_scr[target, chunk * G : (chunk + 1) * G]
                out[1, :, 0] = back_scr[target, chunk * G : (chunk + 1) * G]

    cols = spec((T, BS), lambda b, s: (0, b))
    square = spec((1, BS, BS), lambda b, s: (b, 0, 0))
    piece = jax.ShapeDtypeStruct((2, G, L, SW, T), BF16)
    outs = pl.pallas_call(
        kernel,
        name="enter",
        grid_spec=pltpu.PrefetchScalarGridSpec(
            num_scalar_prefetch=1,
            grid=(L,),
            in_specs=[cols, square, cols, square],
            out_specs=[spec((1, Q, 2, rows, T), lambda b, s: (b, 0, 0, 0, 0))]
            + [spec((2, G, 1, SW, T), lambda b, s: (0, 0, b, 0, 0))] * (N_CHUNK * NT),
            scratch_shapes=[pltpu.VMEM((NT, L, SW, T), BF16)] * 2,
        ),
        out_shape=[jax.ShapeDtypeStruct((L, Q, 2, rows, T), BF16)] + [piece] * (N_CHUNK * NT),
        compiler_params=params(),
    )(where, tokens, up_first, cotangent, down_second)
    return outs[0], [outs[1 + c * NT : 1 + (c + 1) * NT] for c in range(N_CHUNK)]


def middle(where, received, up_second, down_first, chunk, scale, sizes):
    T, L, BS, NT, G, SW, Q, HB = sizes
    rows_up, rows_down = BS // (2 * Q), HB // (2 * Q)
    tile = min(512, HB)

    def kernel(where_ref, *refs):
        ins, up_ref, down_ref = refs[:NT], refs[NT], refs[NT + 1]
        downs, backs = refs[NT + 2 : 2 * NT + 2], refs[2 * NT + 2 : 3 * NT + 2]
        up_send, up_keep, down_send, down_keep = refs[3 * NT + 2 : 3 * NT + 6]
        r_scr, g_scr, rs_scr, act_scr, gp_scr, out_scr = refs[3 * NT + 6 :]
        me, core = where_ref[0], where_ref[1]
        for shift in range(NT):
            source = lax.rem(me + NT - shift, NT)
            r_scr[source] = ins[shift][0, 0].reshape(L * SW, T)
            g_scr[source] = ins[shift][1, 0].reshape(L * SW, T)
        regrouped = r_scr[...].reshape(BS, T)
        grad_mid = g_scr[...].reshape(BS, T)
        rs_scr[...] = regrouped.reshape(Q, 2, rows_up, T)
        for start in range(0, HB, tile):
            pre = dot(up_ref[0, :, start : start + tile], regrouped, 0, 0)
            value, slope = gelu_pair(pre)
            act_scr[start : start + tile] = value.astype(BF16)
            grad_act = dot(down_ref[0, start : start + tile], grad_mid, 1, 0)
            gp_scr[start : start + tile] = (grad_act * slope).astype(BF16)
        activated = act_scr[...]
        grad_pre = gp_scr[...]
        out_scr[0] = dot(down_ref[0], activated, 0, 0).astype(BF16).reshape(NT, L, SW, T)
        out_scr[1] = dot(up_ref[0], grad_pre, 1, 0).astype(BF16).reshape(NT, L, SW, T)
        for shift in range(NT):
            target = lax.rem(me + shift, NT)
            downs[shift][0] = out_scr[0, target]
            backs[shift][0] = out_scr[1, target]
        for send, ref in ((True, up_send), (False, up_keep)):
            half = rs_scr[:, 1 - core if send else core].reshape(Q * rows_up, T)
            part = scale * dot(half, grad_pre, 1, 1)
            ref[0] = part.astype(BF16).reshape(Q, rows_up, HB)
        for send, ref in ((True, down_send), (False, down_keep)):
            for q in range(Q):
                first = (2 * q + (1 - core if send else core)) * rows_down
                half = act_scr[pl.ds(pl.multiple_of(first, rows_down), rows_down)]
                ref[0, q] = (scale * dot(half, grad_mid, 1, 1)).astype(BF16)

    base = chunk * G
    piece = jax.ShapeDtypeStruct((G, L, SW, T), BF16)
    piece_spec = spec((1, L, SW, T), lambda g, s: (g, 0, 0, 0))
    up_part = jax.ShapeDtypeStruct((G, Q, rows_up, HB), BF16)
    down_part = jax.ShapeDtypeStruct((G, Q, rows_down, BS), BF16)
    outs = pl.pallas_call(
        kernel,
        name="middle",
        grid_spec=pltpu.PrefetchScalarGridSpec(
            num_scalar_prefetch=1,
            grid=(G,),
            in_specs=[spec((2, 1, L, SW, T), lambda g, s: (0, g, 0, 0, 0))] * NT
            + [
                spec((1, BS, HB), lambda g, s: (base + g, 0, 0)),
                spec((1, HB, BS), lambda g, s: (base + g, 0, 0)),
            ],
            out_specs=[piece_spec] * (2 * NT)
            + [spec((1, Q, rows_up, HB), lambda g, s: (g, 0, 0, 0))] * 2
            + [spec((1, Q, rows_down, BS), lambda g, s: (g, 0, 0, 0))] * 2,
            scratch_shapes=[
                pltpu.VMEM((NT, L * SW, T), BF16),
                pltpu.VMEM((NT, L * SW, T), BF16),
                pltpu.VMEM((Q, 2, rows_up, T), BF16),
                pltpu.VMEM((HB, T), BF16),
                pltpu.VMEM((HB, T), BF16),
                pltpu.VMEM((2, NT, L, SW, T), BF16),
            ],
        ),
        out_shape=[piece] * (2 * NT) + [up_part] * 2 + [down_part] * 2,
        compiler_params=params(),
    )(where, *received, up_second, down_first)
    return outs[:NT], outs[NT : 2 * NT], outs[2 * NT : 2 * NT + 2], outs[2 * NT + 2 :]


def leave(where, received, weight, base_rows, left, scale, sizes, backward):
    T, L, BS, NT, G, SW, Q, _ = sizes
    rows = BS // (2 * Q)
    n_in = N_CHUNK * NT

    def kernel(where_ref, *refs):
        ins, w_ref, base_ref, left_ref = refs[:n_in], refs[n_in], refs[n_in + 1], refs[n_in + 2]
        out_ref, send_ref, keep_ref, scr, slab_scr = refs[n_in + 3 :]
        me, core = where_ref[0], where_ref[1]
        for shift in range(NT):
            source = lax.rem(me + NT - shift, NT)
            for chunk in range(N_CHUNK):
                scr[source, chunk] = ins[chunk * NT + shift][:, 0]
        regrouped = scr[...].reshape(BS, T)
        if backward:
            branch = dot(regrouped.T, w_ref[0], 1, 1)
        else:
            branch = dot(regrouped, w_ref[0], 0, 0)
            slab_scr[...] = regrouped.reshape(Q, 2, rows, T)
        out_ref[...] = (base_ref[...].astype(F32) + branch).astype(BF16)
        for send, ref in ((True, send_ref), (False, keep_ref)):
            which = 1 - core if send else core
            if backward:
                half = left_ref[0, :, which].reshape(Q * rows, T)
                part = dot(half, regrouped, 1, 1)
            else:
                half = slab_scr[:, which].reshape(Q * rows, T)
                part = dot(half, left_ref[...], 1, 0)
            ref[0] = (scale * part).astype(BF16).reshape(Q, rows, BS)

    cols = spec((T, BS), lambda b, s: (0, b))
    part = jax.ShapeDtypeStruct((L, Q, rows, BS), BF16)
    part_spec = spec((1, Q, rows, BS), lambda b, s: (b, 0, 0, 0))
    left_spec = spec((1, Q, 2, rows, T), lambda b, s: (b, 0, 0, 0, 0)) if backward else cols
    return pl.pallas_call(
        kernel,
        name="leave_back" if backward else "leave_out",
        grid_spec=pltpu.PrefetchScalarGridSpec(
            num_scalar_prefetch=1,
            grid=(L,),
            in_specs=[spec((G, 1, SW, T), lambda b, s: (0, b, 0, 0))] * n_in
            + [spec((1, BS, BS), lambda b, s: (b, 0, 0)), cols, left_spec],
            out_specs=[cols, part_spec, part_spec],
            scratch_shapes=[
                pltpu.VMEM((NT, N_CHUNK, G, SW, T), BF16),
                pltpu.VMEM((Q, 2, rows, T), BF16),
            ],
        ),
        out_shape=[jax.ShapeDtypeStruct((T, L * BS), BF16), part, part],
        compiler_params=params(),
    )(where, *received, weight, base_rows, left)


def shifted(pieces):
    count = len(pieces)
    order = sorted(range(1, count), key=lambda k: -min(k, count - k))
    moved = {k: lax.ppermute(pieces[k], "tensor", [(s, (s + k) % count) for s in range(count)]) for k in order}
    return [pieces[0]] + [moved[k] for k in range(1, count)]


def swap(value, bit):
    count = lax.axis_size("dp")
    return lax.ppermute(value, "dp", [(s, s ^ (1 << bit)) for s in range(count)])


def reduce_parts(send, keep, rising):
    bits = (lax.axis_size("dp") // 2).bit_length() - 1
    order = list(range(bits)) if rising else list(range(bits))[::-1]
    index = lax.axis_index("dp")
    got = swap(send, 0)
    lead, rows, width = keep.shape[0], keep.shape[2], keep.shape[3]
    held = list(range(bits))[::-1]
    keep = keep.reshape((lead,) + (2,) * bits + (rows, width))
    got = got.reshape(keep.shape)
    for bit in order:
        axis = 1 + held.index(bit)
        held.remove(bit)
        mine = (index >> (bit + 1)) & 1

        def pick(which):
            a = lax.dynamic_index_in_dim(keep, which, axis, False).astype(F32)
            b = lax.dynamic_index_in_dim(got, which, axis, False).astype(F32)
            return (a + b).astype(BF16)

        outgoing, staying = pick(1 - mine), pick(mine)
        got = swap(outgoing, bit + 1)
        keep = staying
    return keep.astype(F32) + got.astype(F32)


def body(tokens, up_first, up_second, down_first, down_second, cotangent):
    T = tokens.shape[0]
    L, BS = up_first.shape[0], up_first.shape[1]
    HB = up_second.shape[2]
    NT = lax.axis_size("tensor")
    n_dp = lax.axis_size("dp")
    scale = (T * n_dp) ** (-0.5)
    sizes = (T, L, BS, NT, L // N_CHUNK, BS // NB, n_dp // 2, HB)
    where = jnp.stack([lax.axis_index("tensor"), lax.axis_index("dp") % 2]).astype(jnp.int32)

    x_turned, first = enter(where, tokens, up_first, cotangent, down_second, sizes)
    arrived = [shifted(first[c]) for c in range(N_CHUNK)]
    downs, backs, second, third = [], [], [], []
    for c in range(N_CHUNK):
        down, back, up_parts, down_parts = middle(where, arrived[c], up_second, down_first, c, scale, sizes)
        backs += shifted(back)
        downs += shifted(down)
        second.append(reduce_parts(*up_parts, True))
        third.append(reduce_parts(*down_parts, False))
    grad_tokens, *first_parts = leave(where, backs, up_first, cotangent, x_turned, scale, sizes, True)
    layer_out, *fourth_parts = leave(where, downs, down_second, tokens, cotangent, scale, sizes, False)

    def halves(parts):
        cut = L // 2
        return jnp.concatenate(
            [
                reduce_parts(parts[0][:cut], parts[1][:cut], True),
                reduce_parts(parts[0][cut:], parts[1][cut:], False),
            ]
        )

    return (
        layer_out,
        grad_tokens,
        halves(first_parts),
        jnp.concatenate(second),
        jnp.concatenate(third),
        halves(fourth_parts),
    )


def solution(mesh):
    in_specs = (
        P("dp", "tensor"),
        P("tensor", None, None),
        P("tensor", None, None),
        P("tensor", None, None),
        P("tensor", None, None),
        P("dp", "tensor"),
    )
    out_specs = (
        P("dp", "tensor"),
        P("dp", "tensor"),
        P("tensor", "dp", None),
        P("tensor", "dp", None),
        P("tensor", "dp", None),
        P("tensor", "dp", None),
    )
    return jax.shard_map(body, mesh=mesh, in_specs=in_specs, out_specs=out_specs, check_vma=False)
```

```python
import jax
import jax.numpy as jnp
from jax import lax
from jax.experimental import pallas as pl
from jax.experimental.pallas import tpu as pltpu
from jax.sharding import PartitionSpec as P

NB = 16
N_CHUNK = 2

gelu_coeff = 0.7978845608028654
cubic_coeff = 0.044715

BF16 = jnp.bfloat16
F32 = jnp.float32


def gelu_pair(hidden):
    inner_arg = gelu_coeff * (hidden + cubic_coeff * hidden * hidden * hidden)
    tangent = jnp.tanh(inner_arg)
    gelu_value = 0.5 * hidden * (1.0 + tangent)
    gelu_slope = 0.5 * (1.0 + tangent) + 0.5 * hidden * (1.0 - tangent * tangent) * gelu_coeff * (
        1.0 + 3.0 * cubic_coeff * hidden * hidden
    )
    return gelu_value, gelu_slope


def dot(a, b, ca, cb):
    return lax.dot_general(a, b, (((ca,), (cb,)), ((), ())), preferred_element_type=F32)


def params(mebibytes):
    return pltpu.CompilerParams(vmem_limit_bytes=mebibytes * 1024 * 1024)


def held(*values):
    return [pltpu.with_memory_space_constraint(v, pltpu.HBM) for v in values]


def spec(block, index_map):
    return pl.BlockSpec(block, index_map)


LIGHT = pl.CostEstimate(flops=0, transcendentals=0, bytes_accessed=0)


def enter(tokens, up_first, cotangent, down_second, sizes):
    T, L, BS, NT, G, SW, Q, _ = sizes
    rows = BS // (2 * Q)

    def kernel(x_ref, w_ref, g_ref, d_ref, xt_ref, *outs):
        turned = x_ref[...].T
        xt_ref[0] = turned.reshape(Q, 2, rows, T)
        up = dot(w_ref[0], turned, 0, 0).astype(BF16).reshape(NT, L, SW, T)
        back = dot(d_ref[0], g_ref[...], 1, 1).astype(BF16).reshape(NT, L, SW, T)
        for chunk in range(N_CHUNK):
            outs[chunk][:, 0, :, 0] = up[:, chunk * G : (chunk + 1) * G]
            outs[chunk][:, 1, :, 0] = back[:, chunk * G : (chunk + 1) * G]

    cols = spec((T, BS), lambda b: (0, b))
    square = spec((1, BS, BS), lambda b: (b, 0, 0))
    outs = pl.pallas_call(
        kernel,
        name="enter",
        grid=(L,),
        in_specs=[cols, square, cols, square],
        out_specs=[spec((1, Q, 2, rows, T), lambda b: (b, 0, 0, 0, 0))]
        + [spec((NT, 2, G, 1, SW, T), lambda b: (0, 0, 0, b, 0, 0))] * N_CHUNK,
        out_shape=[pltpu.HBM((L, Q, 2, rows, T), BF16)]
        + [pltpu.HBM((NT, 2, G, L, SW, T), BF16)] * N_CHUNK,
        compiler_params=params(56),
        cost_estimate=LIGHT,
    )(*held(tokens, up_first, cotangent, down_second))
    return outs[0], outs[1:]


def middle(where, received, up_second, down_first, chunk, scale, sizes, joint):
    T, L, BS, NT, G, SW, Q, HB = sizes
    rows_up, rows_down = BS // (2 * Q), HB // (2 * Q)
    tile = min(512, HB)

    def kernel(where_ref, *refs):
        in_ref, up_ref, down_ref = refs[:3]
        up_send, up_keep, down_send, down_keep, rs_scr, act_scr, at_scr, gp_scr = refs[-8:]
        if joint:
            down_out, back_out = refs[3].at[:, 0], refs[3].at[:, 1]
        else:
            down_out, back_out = refs[3:5]
        core = where_ref[0]
        regrouped = in_ref[:, 0, 0].reshape(BS, T)
        rs_scr[...] = regrouped.reshape(Q, 2, rows_up, T)
        turned = regrouped.T
        grad_mid = in_ref[:, 1, 0].reshape(BS, T).T
        for start in range(0, HB, tile):
            pre = dot(turned, up_ref[0, :, start : start + tile], 1, 0)
            value, slope = gelu_pair(pre)
            value = value.astype(BF16)
            act_scr[:, start : start + tile] = value
            at_scr[start : start + tile] = value.T
            grad_act = dot(grad_mid, down_ref[0, start : start + tile], 1, 1)
            gp_scr[:, start : start + tile] = (grad_act * slope).astype(BF16)
        activated = act_scr[...]
        grad_pre = gp_scr[...]
        down_out[:, 0] = dot(activated, down_ref[0], 1, 0).astype(BF16).T.reshape(NT, L, SW, T)
        back_out[:, 0] = dot(grad_pre, up_ref[0], 1, 1).astype(BF16).T.reshape(NT, L, SW, T)
        for send, ref in ((True, up_send), (False, up_keep)):
            half = rs_scr[:, 1 - core if send else core].reshape(Q * rows_up, T)
            part = scale * dot(half, grad_pre, 1, 0)
            ref[0] = part.astype(BF16).reshape(Q, rows_up, HB)
        for send, ref in ((True, down_send), (False, down_keep)):
            for q in range(Q):
                first = (2 * q + (1 - core if send else core)) * rows_down
                half = at_scr[pl.ds(pl.multiple_of(first, rows_down), rows_down)]
                ref[0, q] = (scale * dot(half, grad_mid, 1, 0)).astype(BF16)

    base = chunk * G
    if joint:
        pieces = [pltpu.HBM((NT, 2, G, L, SW, T), BF16)]
        piece_specs = [spec((NT, 2, 1, L, SW, T), lambda g, s: (0, 0, g, 0, 0, 0))]
    else:
        pieces = [pltpu.HBM((NT, G, L, SW, T), BF16)] * 2
        piece_specs = [spec((NT, 1, L, SW, T), lambda g, s: (0, g, 0, 0, 0))] * 2
    up_part = pltpu.HBM((G, Q, rows_up, HB), BF16)
    down_part = pltpu.HBM((G, Q, rows_down, BS), BF16)
    outs = pl.pallas_call(
        kernel,
        name="middle",
        grid_spec=pltpu.PrefetchScalarGridSpec(
            num_scalar_prefetch=1,
            grid=(G,),
            in_specs=[
                spec((NT, 2, 1, L, SW, T), lambda g, s: (0, 0, g, 0, 0, 0)),
                spec((1, BS, HB), lambda g, s: (base + g, 0, 0)),
                spec((1, HB, BS), lambda g, s: (base + g, 0, 0)),
            ],
            out_specs=piece_specs
            + [spec((1, Q, rows_up, HB), lambda g, s: (g, 0, 0, 0))] * 2
            + [spec((1, Q, rows_down, BS), lambda g, s: (g, 0, 0, 0))] * 2,
            scratch_shapes=[
                pltpu.VMEM((Q, 2, rows_up, T), BF16),
                pltpu.VMEM((T, HB), BF16),
                pltpu.VMEM((HB, T), BF16),
                pltpu.VMEM((T, HB), BF16),
            ],
        ),
        out_shape=pieces + [up_part] * 2 + [down_part] * 2,
        compiler_params=params(32),
        cost_estimate=LIGHT,
    )(where, *held(received, up_second, down_first))
    return outs[:-4], outs[-4:-2], outs[-2:]


def leave(where, received, weight, base_rows, left, scale, sizes, backward):
    T, L, BS, NT, G, SW, Q, _ = sizes
    rows = BS // (2 * Q)

    def kernel(where_ref, *refs):
        ins, (w_ref, base_ref, left_ref) = refs[:N_CHUNK], refs[N_CHUNK : N_CHUNK + 3]
        out_ref, send_ref, keep_ref, scr, slab_scr = refs[N_CHUNK + 3 :]
        core = where_ref[0]
        scr[:, 0] = ins[0][:, 0, :, 0]
        scr[:, 1] = ins[1][:, :, 0]
        regrouped = scr[...].reshape(BS, T)
        if backward:
            branch = dot(regrouped.T, w_ref[0], 1, 1)
        else:
            branch = dot(regrouped, w_ref[0], 0, 0)
            slab_scr[...] = regrouped.reshape(Q, 2, rows, T)
        out_ref[...] = (base_ref[...].astype(F32) + branch).astype(BF16)
        for send, ref in ((True, send_ref), (False, keep_ref)):
            which = 1 - core if send else core
            if backward:
                half = left_ref[0, :, which].reshape(Q * rows, T)
                part = dot(half, regrouped, 1, 1)
            else:
                half = slab_scr[:, which].reshape(Q * rows, T)
                part = dot(half, left_ref[...], 1, 0)
            ref[0] = (scale * part).astype(BF16).reshape(Q, rows, BS)

    side = 1 if backward else 0
    cols = spec((T, BS), lambda b, s: (0, b))
    part = jax.ShapeDtypeStruct((L, Q, rows, BS), BF16)
    part_spec = spec((1, Q, rows, BS), lambda b, s: (b, 0, 0, 0))
    left_spec = spec((1, Q, 2, rows, T), lambda b, s: (b, 0, 0, 0, 0)) if backward else cols
    return pl.pallas_call(
        kernel,
        name="leave_back" if backward else "leave_out",
        grid_spec=pltpu.PrefetchScalarGridSpec(
            num_scalar_prefetch=1,
            grid=(L,),
            in_specs=[
                spec((NT, 1, G, 1, SW, T), lambda b, s: (0, side, 0, b, 0, 0)),
                spec((NT, G, 1, SW, T), lambda b, s: (0, 0, b, 0, 0)),
                spec((1, BS, BS), lambda b, s: (b, 0, 0)),
                cols,
                left_spec,
            ],
            out_specs=[cols, part_spec, part_spec],
            scratch_shapes=[
                pltpu.VMEM((NT, N_CHUNK, G, SW, T), BF16),
                pltpu.VMEM((Q, 2, rows, T), BF16),
            ],
        ),
        out_shape=[pltpu.HBM((T, L * BS), BF16), part, part],
        compiler_params=params(24),
        cost_estimate=LIGHT,
    )(where, *held(*received, weight, base_rows, left))


def together(*values):
    return lax.optimization_barrier(values)


def regroup(pieces, label):
    with jax.named_scope(label):
        return lax.all_to_all(pieces, "tensor", split_axis=0, concat_axis=0, tiled=True)


def swap(value, bit, label):
    count = lax.axis_size("dp")
    with jax.named_scope(label):
        return lax.ppermute(value, "dp", [(s, s ^ (1 << bit)) for s in range(count)])


def split(which, pairs, sizes):
    lead, count = sizes
    n = len(pairs)

    def kernel(which_ref, *refs):
        ins, outs = refs[: 4 * n], refs[4 * n :]
        for i in range(2 * n):
            a, b = ins[2 * i][...].astype(F32), ins[2 * i + 1][...].astype(F32)
            outs[i][...] = (a + b).astype(BF16)

    in_specs, operands, out_specs, out_shape = [], [], [], []
    for i, (keep, got, first, place) in enumerate(pairs):
        rows, width = keep.shape[2:]
        for stays in (0, 1):

            def index(a, r, which_ref, i=i, first=first, place=place, stays=stays):
                mine = which_ref[i]
                chosen = mine if stays else 1 - mine
                low = r & ((1 << place) - 1)
                return (first + a, ((r >> place) << (place + 1)) | (chosen << place) | low, 0, 0)

            in_specs += [spec((1, 1, rows, width), index)] * 2
            operands += [keep, got]
            out_specs.append(spec((1, 1, rows, width), lambda a, r, w: (a, r, 0, 0)))
            out_shape.append(pltpu.HBM((lead, count // 2, rows, width), BF16))
    outs = pl.pallas_call(
        kernel,
        name="split",
        grid_spec=pltpu.PrefetchScalarGridSpec(
            num_scalar_prefetch=1, grid=(lead, count // 2), in_specs=in_specs, out_specs=out_specs
        ),
        out_shape=out_shape,
        compiler_params=params(16),
        cost_estimate=LIGHT,
    )(which, *held(*operands))
    return [(outs[2 * i], outs[2 * i + 1]) for i in range(n)]


def whole():
    return pl.BlockSpec(memory_space=pltpu.VMEM)


def split_small(which, pairs, lead):
    n = len(pairs)

    def kernel(which_ref, *refs):
        ins, outs = refs[: 2 * n], refs[2 * n :]
        for i, (keep, _, first, place) in enumerate(pairs):
            for stays in (0, 1):
                chosen = which_ref[i] if stays else 1 - which_ref[i]
                for r in range(keep.shape[1] // 2):
                    low = r & ((1 << place) - 1)
                    q = ((r >> place) << (place + 1)) + low + chosen * (1 << place)
                    for a in range(lead):
                        total = ins[2 * i][first + a, q].astype(F32) + ins[2 * i + 1][first + a, q].astype(F32)
                        outs[2 * i + stays][a, r] = total.astype(BF16)

    out_shape = []
    for keep, _, _, _ in pairs:
        out_shape += [jax.ShapeDtypeStruct((lead, keep.shape[1] // 2) + keep.shape[2:], BF16)] * 2
    outs = pl.pallas_call(
        kernel,
        name="small",
        in_specs=[pl.BlockSpec(memory_space=pltpu.SMEM)] + [whole()] * (2 * n),
        out_specs=[whole()] * (2 * n),
        out_shape=out_shape,
        compiler_params=params(8),
        cost_estimate=LIGHT,
    )(which, *[array for keep, got, _, _ in pairs for array in (keep, got)])
    return [(outs[2 * i], outs[2 * i + 1]) for i in range(n)]


def finish(groups):
    n = len(groups)
    lead = groups[0][0].shape[0]

    def kernel(*refs):
        ins, outs = refs[: 4 * n], refs[4 * n :]
        for i in range(n):
            for j in range(2):
                a, b = ins[4 * i + 2 * j], ins[4 * i + 2 * j + 1]
                outs[i][j * lead : (j + 1) * lead] = a[:, 0].astype(F32) + b[:, 0].astype(F32)

    return pl.pallas_call(
        kernel,
        name="finish",
        in_specs=[whole()] * (4 * n),
        out_shape=[jax.ShapeDtypeStruct((2 * lead,) + group[0].shape[2:], F32) for group in groups],
        compiler_params=params(16),
        cost_estimate=LIGHT,
    )(*[array for group in groups for array in group])


class Halving:
    def __init__(self, streams, label, large):
        self.label = label
        self.large = large
        self.bits = bits = (lax.axis_size("dp") // 2).bit_length() - 1
        self.orders = [list(range(bits)), list(range(bits))[::-1]]
        self.held = [list(range(bits)), list(range(bits))]
        self.streams = streams

    def add(self, lead):
        index = lax.axis_index("dp")
        pairs, mine = [], []
        self.moving = []
        for (keep, got, first), order, held in zip(self.streams, self.orders, self.held):
            bit = order.pop(0)
            pairs.append((keep, got, first, held.index(bit)))
            held.remove(bit)
            mine.append((index >> (bit + 1)) & 1)
            self.moving.append(bit)
        which = jnp.stack(mine).astype(jnp.int32)
        if self.large and len(self.held[0]) == self.bits - 1:
            self.parts = split(which, pairs, (lead, pairs[0][0].shape[1]))
        else:
            self.parts = split_small(which, pairs, lead)
        return [outgoing for outgoing, _ in self.parts]

    def move(self, outgoing):
        self.streams = [
            (staying, swap(out, bit + 1, "%s_bit%d" % (self.label, bit)), 0)
            for out, (_, staying), bit in zip(outgoing, self.parts, self.moving)
        ]

    def got(self):
        return [got for _, got, _ in self.streams]

    def replace(self, arrived):
        self.streams = [(keep, got, first) for (keep, _, first), got in zip(self.streams, arrived)]

    def run(self, lead):
        while self.orders[0]:
            self.move(self.add(lead))
        return [(keep, got) for keep, got, _ in self.streams]


def body(tokens, up_first, up_second, down_first, down_second, cotangent):
    T = tokens.shape[0]
    L, BS = up_first.shape[0], up_first.shape[1]
    HB = up_second.shape[2]
    NT = lax.axis_size("tensor")
    n_dp = lax.axis_size("dp")
    scale = (T * n_dp) ** (-0.5)
    sizes = (T, L, BS, NT, L // N_CHUNK, BS // NB, n_dp // 2, HB)
    where = (lax.axis_index("dp") % 2).astype(jnp.int32).reshape(1)

    lead = L // N_CHUNK

    def middle_sums(parts, label, before):
        (up_send, up_keep), (down_send, down_keep) = parts
        if before is not None:
            up_send, down_send, *got = together(up_send, down_send, *before.got())
            before.replace(got)
        got_up, got_down = swap(up_send, 0, label + "_core"), swap(down_send, 0, label + "_core")
        return Halving([(up_keep, got_up, 0), (down_keep, got_down, 0)], label, True)

    def edge_sums(parts, label):
        send, keep = parts
        got = swap(send, 0, label + "_core")
        return Halving([(keep, got, 0), (keep, got, lead)], label, False)

    x_turned, (first_0, first_1) = enter(tokens, up_first, cotangent, down_second, sizes)
    in_0 = regroup(first_0, "z1")
    in_0, first_1 = together(in_0, first_1)
    in_1 = regroup(first_1, "z2")
    (both_0,), *parts = middle(where, in_0, up_second, down_first, 0, scale, sizes, True)
    mid_0 = middle_sums(parts, "mid0", None)
    leaving_0 = mid_0.add(lead)
    in_1, both_0 = together(in_1, both_0)
    both_0 = regroup(both_0, "z3")
    mid_0.move(leaving_0)
    in_1, *_ = together(in_1, *leaving_0)
    (down_1, back_1), *parts = middle(where, in_1, up_second, down_first, 1, scale, sizes, False)
    mid_1 = middle_sums(parts, "mid1", mid_0)
    leaving_0 = mid_0.add(lead)
    leaving_1 = mid_1.add(lead)
    both_0, back_1, *_ = together(both_0, back_1, *leaving_0)
    back_1 = regroup(back_1, "z4")
    mid_0.move(leaving_0)
    mid_1.move(leaving_1)
    back_1, down_1, *got = together(back_1, down_1, *mid_0.got(), *leaving_1)
    mid_0.replace(got[:2])
    down_1 = regroup(down_1, "z5")
    grad_tokens, *parts = leave(
        where, (both_0, back_1), up_first, cotangent, x_turned, scale, sizes, True
    )
    edge_first = edge_sums(parts, "first")
    leaving_first = edge_first.add(lead)
    leaving_1 = mid_1.add(lead) if mid_1.orders[0] else []
    edge_first.move(leaving_first)
    mid_1.move(leaving_1)
    down_1, *_ = together(down_1, *leaving_first, *leaving_1)
    layer_out, *parts = leave(
        where, (both_0, down_1), down_second, tokens, cotangent, scale, sizes, False
    )
    edge_fourth = edge_sums(parts, "fourth")
    done_0, done_1 = mid_0.run(lead), mid_1.run(lead)
    leaving_first = edge_first.add(lead)
    edge_fourth.replace(together(*edge_fourth.got(), *leaving_first)[:2])
    edge_first.move(leaving_first)
    leaving_fourth = edge_fourth.add(lead)
    edge_fourth.move(leaving_fourth)
    grad_up_second, grad_down_first = finish([done_0[0] + done_1[0], done_0[1] + done_1[1]])
    (grad_up_first,) = finish([sum(edge_first.run(lead), ())])
    got = together(*edge_fourth.got(), grad_up_second, grad_down_first)
    edge_fourth.replace(got[:2])
    (grad_down_second,) = finish([sum(edge_fourth.run(lead), ())])
    return (
        layer_out,
        grad_tokens,
        grad_up_first.reshape(L, -1, BS),
        got[2].reshape(L, -1, HB),
        got[3].reshape(L, -1, BS),
        grad_down_second.reshape(L, -1, BS),
    )


def solution(mesh):
    in_specs = (
        P("dp", "tensor"),
        P("tensor", None, None),
        P("tensor", None, None),
        P("tensor", None, None),
        P("tensor", None, None),
        P("dp", "tensor"),
    )
    out_specs = (
        P("dp", "tensor"),
        P("dp", "tensor"),
        P("tensor", "dp", None),
        P("tensor", "dp", None),
        P("tensor", "dp", None),
        P("tensor", "dp", None),
    )
    return jax.shard_map(body, mesh=mesh, in_specs=in_specs, out_specs=out_specs, check_vma=False)
```

```python
import jax
import jax.numpy as jnp
from jax import lax
from jax.experimental import pallas as pl
from jax.experimental.pallas import tpu as pltpu
from jax.sharding import PartitionSpec as P

NB = 16
N_CHUNK = 2

gelu_coeff = 0.7978845608028654
cubic_coeff = 0.044715

BF16 = jnp.bfloat16
F32 = jnp.float32


def gelu_pair(hidden):
    inner_arg = gelu_coeff * (hidden + cubic_coeff * hidden * hidden * hidden)
    tangent = jnp.tanh(inner_arg)
    gelu_value = 0.5 * hidden * (1.0 + tangent)
    gelu_slope = 0.5 * (1.0 + tangent) + 0.5 * hidden * (1.0 - tangent * tangent) * gelu_coeff * (
        1.0 + 3.0 * cubic_coeff * hidden * hidden
    )
    return gelu_value, gelu_slope


def dot(a, b, ca, cb):
    return lax.dot_general(a, b, (((ca,), (cb,)), ((), ())), preferred_element_type=F32)


def params(mebibytes):
    return pltpu.CompilerParams(vmem_limit_bytes=mebibytes * 1024 * 1024)


def held(*values):
    return [pltpu.with_memory_space_constraint(v, pltpu.HBM) for v in values]


def spec(block, index_map):
    return pl.BlockSpec(block, index_map)


LIGHT = pl.CostEstimate(flops=0, transcendentals=0, bytes_accessed=0)


def enter(tokens, up_first, cotangent, down_second, sizes):
    T, L, BS, NT, G, SW, Q, _ = sizes

    def kernel(x_ref, w_ref, g_ref, d_ref, *outs):
        up = dot(x_ref[...], w_ref[0], 1, 0).astype(BF16).T.reshape(NT, L, SW, T)
        back = dot(d_ref[0], g_ref[...], 1, 1).astype(BF16).reshape(NT, L, SW, T)
        for chunk in range(N_CHUNK):
            outs[chunk][:, 0, :, 0] = up[:, chunk * G : (chunk + 1) * G]
            outs[chunk][:, 1, :, 0] = back[:, chunk * G : (chunk + 1) * G]

    cols = spec((T, BS), lambda b: (0, b))
    square = spec((1, BS, BS), lambda b: (b, 0, 0))
    outs = pl.pallas_call(
        kernel,
        name="enter",
        grid=(L,),
        in_specs=[cols, square, cols, square],
        out_specs=[spec((NT, 2, G, 1, SW, T), lambda b: (0, 0, 0, b, 0, 0))] * N_CHUNK,
        out_shape=[pltpu.HBM((NT, 2, G, L, SW, T), BF16)] * N_CHUNK,
        compiler_params=params(56),
        cost_estimate=LIGHT,
    )(*held(tokens, up_first, cotangent, down_second))
    return outs


def turn(tokens, sizes):
    T, L, BS, _, _, _, Q, _ = sizes
    rows = BS // (2 * Q)

    def kernel(x_ref, out_ref):
        out_ref[0] = x_ref[...].T.reshape(Q, 2, rows, T)

    return pl.pallas_call(
        kernel,
        name="turn",
        grid=(L,),
        in_specs=[spec((T, BS), lambda b: (0, b))],
        out_specs=spec((1, Q, 2, rows, T), lambda b: (b, 0, 0, 0, 0)),
        out_shape=pltpu.HBM((L, Q, 2, rows, T), BF16),
        compiler_params=params(56),
        cost_estimate=LIGHT,
    )(*held(tokens))


def middle(where, received, up_second, down_first, chunk, scale, sizes, joint):
    T, L, BS, NT, G, SW, Q, HB = sizes
    rows_up, rows_down = BS // (2 * Q), HB // (2 * Q)
    cut = max(L // 4, 1)
    tile = min(512, HB)

    def kernel(where_ref, *refs):
        in_ref, up_ref, down_ref = refs[:3]
        up_send, up_keep, down_send, down_keep, rs_scr, act_scr, at_scr, gp_scr = refs[-8:]
        core = where_ref[0]
        regrouped = in_ref[:, 0, 0].reshape(BS, T)
        rs_scr[...] = regrouped.reshape(Q, 2, rows_up, T)
        turned = regrouped.T
        grad_mid = in_ref[:, 1, 0].reshape(BS, T).T
        for start in range(0, HB, tile):
            pre = dot(turned, up_ref[0, :, start : start + tile], 1, 0)
            value, slope = gelu_pair(pre)
            value = value.astype(BF16)
            act_scr[:, start : start + tile] = value
            at_scr[start : start + tile] = value.T
            grad_act = dot(grad_mid, down_ref[0, start : start + tile], 1, 1)
            gp_scr[:, start : start + tile] = (grad_act * slope).astype(BF16)
        activated = act_scr[...]
        grad_pre = gp_scr[...]
        down = dot(activated, down_ref[0], 1, 0).astype(BF16).T.reshape(NT, L, SW, T)
        back = dot(grad_pre, up_ref[0], 1, 1).astype(BF16).T.reshape(NT, L, SW, T)
        if joint:
            refs[3][:, 0, :L] = back
            refs[3][:, 0, L:] = down
        else:
            refs[3][:, 0, :L] = back
            refs[3][:, 0, L:] = down[:, :cut]
            refs[4][:, 0] = down[:, cut:]
        for send, ref in ((True, up_send), (False, up_keep)):
            half = rs_scr[:, 1 - core if send else core].reshape(Q * rows_up, T)
            part = scale * dot(half, grad_pre, 1, 0)
            ref[0] = part.astype(BF16).reshape(Q, rows_up, HB)
        for send, ref in ((True, down_send), (False, down_keep)):
            for q in range(Q):
                first = (2 * q + (1 - core if send else core)) * rows_down
                half = at_scr[pl.ds(pl.multiple_of(first, rows_down), rows_down)]
                ref[0, q] = (scale * dot(half, grad_mid, 1, 0)).astype(BF16)

    base = chunk * G
    widths = [2 * L] if joint else [L + cut, L - cut]
    pieces = [pltpu.HBM((NT, G, w, SW, T), BF16) for w in widths]
    piece_specs = [spec((NT, 1, w, SW, T), lambda g, s: (0, g, 0, 0, 0)) for w in widths]
    up_part = pltpu.HBM((G, Q, rows_up, HB), BF16)
    down_part = pltpu.HBM((G, Q, rows_down, BS), BF16)
    outs = pl.pallas_call(
        kernel,
        name="middle",
        grid_spec=pltpu.PrefetchScalarGridSpec(
            num_scalar_prefetch=1,
            grid=(G,),
            in_specs=[
                spec((NT, 2, 1, L, SW, T), lambda g, s: (0, 0, g, 0, 0, 0)),
                spec((1, BS, HB), lambda g, s: (base + g, 0, 0)),
                spec((1, HB, BS), lambda g, s: (base + g, 0, 0)),
            ],
            out_specs=piece_specs
            + [spec((1, Q, rows_up, HB), lambda g, s: (g, 0, 0, 0))] * 2
            + [spec((1, Q, rows_down, BS), lambda g, s: (g, 0, 0, 0))] * 2,
            scratch_shapes=[
                pltpu.VMEM((Q, 2, rows_up, T), BF16),
                pltpu.VMEM((T, HB), BF16),
                pltpu.VMEM((HB, T), BF16),
                pltpu.VMEM((T, HB), BF16),
            ],
        ),
        out_shape=pieces + [up_part] * 2 + [down_part] * 2,
        compiler_params=params(32),
        cost_estimate=LIGHT,
    )(where, *held(received, up_second, down_first))
    return outs[:-4], outs[-4:-2], outs[-2:]


def leave(where, received, places, weight, base_rows, left, scale, sizes, backward, first, count, onto=None):
    T, L, BS, NT, G, SW, Q, _ = sizes
    rows = BS // (2 * Q)

    def kernel(where_ref, *refs):
        ins, (w_ref, base_ref, left_ref) = refs[:N_CHUNK], refs[N_CHUNK : N_CHUNK + 3]
        out_ref, send_ref, keep_ref, scr, slab_scr = refs[-5:]
        core = where_ref[0]
        scr[:, 0] = ins[0][:, :, 0]
        scr[:, 1] = ins[1][:, :, 0]
        regrouped = scr[...].reshape(BS, T)
        if backward:
            branch = dot(regrouped.T, w_ref[0], 1, 1)
        else:
            branch = dot(regrouped, w_ref[0], 0, 0)
            slab_scr[...] = regrouped.reshape(Q, 2, rows, T)
        out_ref[...] = (base_ref[...].astype(F32) + branch).astype(BF16)
        for send, ref in ((True, send_ref), (False, keep_ref)):
            which = 1 - core if send else core
            if backward:
                half = left_ref[0, :, which].reshape(Q * rows, T)
                part = dot(half, regrouped, 1, 1)
            else:
                half = slab_scr[:, which].reshape(Q * rows, T)
                part = dot(half, left_ref[...], 1, 0)
            ref[0] = (scale * part).astype(BF16).reshape(Q, rows, BS)

    cols = spec((T, BS), lambda b, s: (0, first + b))
    part = jax.ShapeDtypeStruct((count, Q, rows, BS), BF16)
    part_spec = spec((1, Q, rows, BS), lambda b, s: (b, 0, 0, 0))
    left_spec = spec((1, Q, 2, rows, T), lambda b, s: (first + b, 0, 0, 0, 0)) if backward else cols
    operands = held(*received, weight, base_rows, left)
    more, aliases = [], {}
    if onto is not None:
        operands += held(onto)
        more, aliases = [pl.BlockSpec(memory_space=pl.ANY)], {N_CHUNK + 4: 0}
    return pl.pallas_call(
        kernel,
        name="leave_back" if backward else "leave_out",
        grid_spec=pltpu.PrefetchScalarGridSpec(
            num_scalar_prefetch=1,
            grid=(count,),
            in_specs=[
                spec((NT, G, 1, SW, T), lambda b, s, place=place: (0, 0, place + b, 0, 0)) for place in places
            ]
            + [spec((1, BS, BS), lambda b, s: (first + b, 0, 0)), cols, left_spec]
            + more,
            out_specs=[cols, part_spec, part_spec],
            scratch_shapes=[
                pltpu.VMEM((NT, N_CHUNK, G, SW, T), BF16),
                pltpu.VMEM((Q, 2, rows, T), BF16),
            ],
        ),
        out_shape=[pltpu.HBM((T, L * BS), BF16), part, part],
        input_output_aliases=aliases,
        compiler_params=params(24),
        cost_estimate=LIGHT,
    )(where, *operands)


def together(*values):
    return lax.optimization_barrier(values)


def regroup(pieces, label):
    with jax.named_scope(label):
        return lax.all_to_all(pieces, "tensor", split_axis=0, concat_axis=0, tiled=True)


def swap(value, bit, label):
    count = lax.axis_size("dp")
    with jax.named_scope(label):
        return lax.ppermute(value, "dp", [(s, s ^ (1 << bit)) for s in range(count)])


def split(which, pairs, sizes):
    lead, count = sizes
    n = len(pairs)

    def kernel(which_ref, *refs):
        ins, outs = refs[: 4 * n], refs[4 * n :]
        for i in range(2 * n):
            a, b = ins[2 * i][...].astype(F32), ins[2 * i + 1][...].astype(F32)
            outs[i][...] = (a + b).astype(BF16)

    in_specs, operands, out_specs, out_shape = [], [], [], []
    for i, (keep, got, first, place) in enumerate(pairs):
        rows, width = keep.shape[2:]
        for stays in (0, 1):

            def index(a, r, which_ref, i=i, first=first, place=place, stays=stays):
                mine = which_ref[i]
                chosen = mine if stays else 1 - mine
                low = r & ((1 << place) - 1)
                return (first + a, ((r >> place) << (place + 1)) | (chosen << place) | low, 0, 0)

            in_specs += [spec((1, 1, rows, width), index)] * 2
            operands += [keep, got]
            out_specs.append(spec((1, 1, rows, width), lambda a, r, w: (a, r, 0, 0)))
            out_shape.append(pltpu.HBM((lead, count // 2, rows, width), BF16))
    outs = pl.pallas_call(
        kernel,
        name="split",
        grid_spec=pltpu.PrefetchScalarGridSpec(
            num_scalar_prefetch=1, grid=(lead, count // 2), in_specs=in_specs, out_specs=out_specs
        ),
        out_shape=out_shape,
        compiler_params=params(16),
        cost_estimate=LIGHT,
    )(which, *held(*operands))
    return [(outs[2 * i], outs[2 * i + 1]) for i in range(n)]


def whole():
    return pl.BlockSpec(memory_space=pltpu.VMEM)


def split_small(which, pairs, lead):
    n = len(pairs)

    def kernel(which_ref, *refs):
        ins, outs = refs[: 2 * n], refs[2 * n :]
        for i, (keep, _, first, place) in enumerate(pairs):
            for stays in (0, 1):
                chosen = which_ref[i] if stays else 1 - which_ref[i]
                for r in range(keep.shape[1] // 2):
                    low = r & ((1 << place) - 1)
                    q = ((r >> place) << (place + 1)) + low + chosen * (1 << place)
                    for a in range(lead):
                        total = ins[2 * i][first + a, q].astype(F32) + ins[2 * i + 1][first + a, q].astype(F32)
                        outs[2 * i + stays][a, r] = total.astype(BF16)

    out_shape = []
    for keep, _, _, _ in pairs:
        out_shape += [jax.ShapeDtypeStruct((lead, keep.shape[1] // 2) + keep.shape[2:], BF16)] * 2
    outs = pl.pallas_call(
        kernel,
        name="small",
        in_specs=[pl.BlockSpec(memory_space=pltpu.SMEM)] + [whole()] * (2 * n),
        out_specs=[whole()] * (2 * n),
        out_shape=out_shape,
        compiler_params=params(8),
        cost_estimate=LIGHT,
    )(which, *[array for keep, got, _, _ in pairs for array in (keep, got)])
    return [(outs[2 * i], outs[2 * i + 1]) for i in range(n)]


def finish(groups):
    shapes = [(sum(keep.shape[0] for keep, _ in pairs),) + pairs[0][0].shape[2:] for pairs in groups]
    n_in = sum(2 * len(pairs) for pairs in groups)

    def kernel(*refs):
        ins, outs = list(refs[:n_in]), refs[n_in:]
        for pairs, out in zip(groups, outs):
            start = 0
            for keep, _ in pairs:
                a, b = ins.pop(0), ins.pop(0)
                out[start : start + keep.shape[0]] = a[:, 0].astype(F32) + b[:, 0].astype(F32)
                start += keep.shape[0]

    return pl.pallas_call(
        kernel,
        name="finish",
        in_specs=[whole()] * n_in,
        out_shape=[jax.ShapeDtypeStruct(shape, F32) for shape in shapes],
        compiler_params=params(16),
        cost_estimate=LIGHT,
    )(*[array for pairs in groups for pair in pairs for array in pair])


class Halving:
    def __init__(self, streams, label, large, turned=0):
        self.label = label
        self.large = large
        self.bits = bits = (lax.axis_size("dp") // 2).bit_length() - 1
        self.orders = [list(range(bits))[:: -1 if (i + turned) % 2 else 1] for i in range(len(streams))]
        self.held = [list(range(bits)) for _ in streams]
        self.streams = streams

    def add(self, lead):
        index = lax.axis_index("dp")
        pairs, mine = [], []
        self.moving = []
        for (keep, got, first), order, held in zip(self.streams, self.orders, self.held):
            bit = order.pop(0)
            pairs.append((keep, got, first, held.index(bit)))
            held.remove(bit)
            mine.append((index >> (bit + 1)) & 1)
            self.moving.append(bit)
        which = jnp.stack(mine).astype(jnp.int32)
        if self.large and len(self.held[0]) == self.bits - 1:
            self.parts = split(which, pairs, (lead, pairs[0][0].shape[1]))
        else:
            self.parts = split_small(which, pairs, lead)
        return [outgoing for outgoing, _ in self.parts]

    def move(self, outgoing):
        self.streams = [
            (staying, swap(out, bit + 1, "%s_bit%d" % (self.label, bit)), 0)
            for out, (_, staying), bit in zip(outgoing, self.parts, self.moving)
        ]

    def got(self):
        return [got for _, got, _ in self.streams]

    def replace(self, arrived):
        self.streams = [(keep, got, first) for (keep, _, first), got in zip(self.streams, arrived)]

    def run(self, lead):
        while self.orders[0]:
            self.move(self.add(lead))
        return [(keep, got) for keep, got, _ in self.streams]


def body(tokens, up_first, up_second, down_first, down_second, cotangent):
    T = tokens.shape[0]
    L, BS = up_first.shape[0], up_first.shape[1]
    HB = up_second.shape[2]
    NT = lax.axis_size("tensor")
    n_dp = lax.axis_size("dp")
    scale = (T * n_dp) ** (-0.5)
    sizes = (T, L, BS, NT, L // N_CHUNK, BS // NB, n_dp // 2, HB)
    where = (lax.axis_index("dp") % 2).astype(jnp.int32).reshape(1)

    lead = L // N_CHUNK
    half = L // 2
    cut = max(L // 4, 1)

    def middle_sums(parts, label, before):
        (up_send, up_keep), (down_send, down_keep) = parts
        if before is not None:
            up_send, down_send, *got = together(up_send, down_send, *before.got())
            before.replace(got)
        got_up, got_down = swap(up_send, 0, label + "_core"), swap(down_send, 0, label + "_core")
        return Halving([(up_keep, got_up, 0), (down_keep, got_down, 0)], label, True)

    first_0, first_1 = enter(tokens, up_first, cotangent, down_second, sizes)
    in_0 = regroup(first_0, "z1")
    x_turned = turn(tokens, sizes)
    in_0, first_1, x_turned = together(in_0, first_1, x_turned)
    in_1 = regroup(first_1, "z2")
    (both_0,), *parts = middle(where, in_0, up_second, down_first, 0, scale, sizes, True)
    mid_0 = middle_sums(parts, "mid0", None)
    leaving_0 = mid_0.add(lead)
    in_1, both_0, *_ = together(in_1, both_0, *leaving_0)
    both_0 = regroup(both_0, "z3")
    mid_0.move(leaving_0)
    (most_1, rest_1), *parts = middle(where, in_1, up_second, down_first, 1, scale, sizes, False)
    mid_1 = middle_sums(parts, "mid1", mid_0)
    leaving_0 = mid_0.add(lead)
    both_0, most_1, *_ = together(both_0, most_1, *leaving_0)
    most_1 = regroup(most_1, "z4")
    mid_0.move(leaving_0)
    got = together(*mid_0.got(), *mid_1.got())
    mid_0.replace(got[:2])
    mid_1.replace(got[2:])
    leaving_1 = mid_1.add(lead)
    mid_1.move(leaving_1)
    most_1, rest_1, *_ = together(most_1, rest_1, *leaving_1)
    rest_1 = regroup(rest_1, "z5")
    grad_tokens, parts = None, []
    for start, count in ((0, half), (half, L - half)):
        grad_tokens, *part = leave(
            where,
            (both_0, most_1),
            (start, start),
            up_first,
            cotangent,
            x_turned,
            scale,
            sizes,
            True,
            start,
            count,
            grad_tokens,
        )
        parts.append(part)
    edge_first = Halving([(keep, swap(send, 0, "first_core"), 0) for send, keep in parts], "first", False)
    layer_out, *low = leave(
        where, (both_0, most_1), (L, L), down_second, tokens, cotangent, scale, sizes, False, 0, cut
    )
    edge_low = Halving([(low[1], swap(low[0], 0, "low_core"), 0)], "low", False)
    leaving_first = edge_first.add(lead)
    leaving_low = edge_low.add(cut)
    leaving_1 = mid_1.add(lead) if mid_1.orders[0] else []
    edge_first.move(leaving_first)
    edge_low.move(leaving_low)
    mid_1.move(leaving_1)
    rest_1, *_ = together(rest_1, *leaving_first, *leaving_low, *leaving_1)
    layer_out, *high = leave(
        where,
        (both_0, rest_1),
        (L + cut, 0),
        down_second,
        tokens,
        cotangent,
        scale,
        sizes,
        False,
        cut,
        L - cut,
        layer_out,
    )
    high[0], *got = together(high[0], *edge_first.got(), *edge_low.got())
    edge_first.replace(got[:2])
    edge_low.replace(got[2:])
    edge_high = Halving([(high[1], swap(high[0], 0, "high_core"), 0)], "high", False, 1)
    edge_high.move(edge_high.add(L - cut))
    done_0, done_1 = mid_0.run(lead), mid_1.run(lead)
    grad_up_second, grad_down_first = finish([[done_0[0], done_1[0]], [done_0[1], done_1[1]]])
    done_first, done_low = edge_first.run(lead), edge_low.run(cut)
    got = together(*edge_high.got(), grad_up_second, grad_down_first)
    edge_high.replace(got[:1])
    done_high = edge_high.run(L - cut)
    (grad_up_first,) = finish([done_first])
    (grad_down_second,) = finish([done_low + done_high])
    return (
        layer_out,
        grad_tokens,
        grad_up_first.reshape(L, -1, BS),
        got[-2].reshape(L, -1, HB),
        got[-1].reshape(L, -1, BS),
        grad_down_second.reshape(L, -1, BS),
    )


def solution(mesh):
    in_specs = (
        P("dp", "tensor"),
        P("tensor", None, None),
        P("tensor", None, None),
        P("tensor", None, None),
        P("tensor", None, None),
        P("dp", "tensor"),
    )
    out_specs = (
        P("dp", "tensor"),
        P("dp", "tensor"),
        P("tensor", "dp", None),
        P("tensor", "dp", None),
        P("tensor", "dp", None),
        P("tensor", "dp", None),
    )
    return jax.shard_map(body, mesh=mesh, in_specs=in_specs, out_specs=out_specs, check_vma=False)
```

```python
import jax
import jax.numpy as jnp
from jax import lax
from jax.experimental import pallas as pl
from jax.experimental.pallas import tpu as pltpu
from jax.sharding import PartitionSpec as P

NB = 16
N_CHUNK = 2

gelu_coeff = 0.7978845608028654
cubic_coeff = 0.044715

BF16 = jnp.bfloat16
F32 = jnp.float32


def gelu_pair(hidden):
    inner_arg = gelu_coeff * (hidden + cubic_coeff * hidden * hidden * hidden)
    tangent = jnp.tanh(inner_arg)
    gelu_value = 0.5 * hidden * (1.0 + tangent)
    gelu_slope = 0.5 * (1.0 + tangent) + 0.5 * hidden * (1.0 - tangent * tangent) * gelu_coeff * (
        1.0 + 3.0 * cubic_coeff * hidden * hidden
    )
    return gelu_value, gelu_slope


def dot(a, b, ca, cb):
    return lax.dot_general(a, b, (((ca,), (cb,)), ((), ())), preferred_element_type=F32)


def params(mebibytes):
    return pltpu.CompilerParams(vmem_limit_bytes=mebibytes * 1024 * 1024)


def held(*values):
    return [pltpu.with_memory_space_constraint(v, pltpu.HBM) for v in values]


def spec(block, index_map):
    return pl.BlockSpec(block, index_map)


LIGHT = pl.CostEstimate(flops=0, transcendentals=0, bytes_accessed=0)


def enter(tokens, up_first, cotangent, down_second, sizes):
    T, L, BS, NT, G, SW, Q, _ = sizes

    def kernel(x_ref, w_ref, g_ref, d_ref, *outs):
        up = dot(x_ref[...], w_ref[0], 1, 0).astype(BF16).T.reshape(NT, L, SW, T)
        back = dot(d_ref[0], g_ref[...], 1, 1).astype(BF16).reshape(NT, L, SW, T)
        for chunk in range(N_CHUNK):
            outs[chunk][:, 0, :, 0] = up[:, chunk * G : (chunk + 1) * G]
            outs[chunk][:, 1, :, 0] = back[:, chunk * G : (chunk + 1) * G]

    cols = spec((T, BS), lambda b: (0, b))
    square = spec((1, BS, BS), lambda b: (b, 0, 0))
    outs = pl.pallas_call(
        kernel,
        name="enter",
        grid=(L,),
        in_specs=[cols, square, cols, square],
        out_specs=[spec((NT, 2, G, 1, SW, T), lambda b: (0, 0, 0, b, 0, 0))] * N_CHUNK,
        out_shape=[pltpu.HBM((NT, 2, G, L, SW, T), BF16)] * N_CHUNK,
        compiler_params=params(56),
        cost_estimate=LIGHT,
    )(*held(tokens, up_first, cotangent, down_second))
    return outs


def turn(tokens, sizes):
    T, L, BS, _, _, _, Q, _ = sizes
    rows = BS // (2 * Q)

    def kernel(x_ref, out_ref):
        out_ref[0] = x_ref[...].T.reshape(Q, 2, rows, T)

    return pl.pallas_call(
        kernel,
        name="turn",
        grid=(L,),
        in_specs=[spec((T, BS), lambda b: (0, b))],
        out_specs=spec((1, Q, 2, rows, T), lambda b: (b, 0, 0, 0, 0)),
        out_shape=pltpu.HBM((L, Q, 2, rows, T), BF16),
        compiler_params=params(56),
        cost_estimate=LIGHT,
    )(*held(tokens))


def middle(where, received, up_second, down_first, chunk, scale, sizes, joint):
    T, L, BS, NT, G, SW, Q, HB = sizes
    rows_up, rows_down = BS // (2 * Q), HB // (2 * Q)
    cut = max(L // 4, 1)
    tile = min(512, HB)

    def kernel(where_ref, *refs):
        in_ref, up_ref, down_ref = refs[:3]
        up_send, up_keep, down_send, down_keep, rs_scr, act_scr, at_scr, gp_scr = refs[-8:]
        core = where_ref[0]
        regrouped = in_ref[:, 0, 0].reshape(BS, T)
        rs_scr[...] = regrouped.reshape(Q, 2, rows_up, T)
        turned = regrouped.T
        grad_mid = in_ref[:, 1, 0].reshape(BS, T).T
        for start in range(0, HB, tile):
            pre = dot(turned, up_ref[0, :, start : start + tile], 1, 0)
            value, slope = gelu_pair(pre)
            value = value.astype(BF16)
            act_scr[:, start : start + tile] = value
            at_scr[start : start + tile] = value.T
            grad_act = dot(grad_mid, down_ref[0, start : start + tile], 1, 1)
            gp_scr[:, start : start + tile] = (grad_act * slope).astype(BF16)
        activated = act_scr[...]
        grad_pre = gp_scr[...]
        down = dot(activated, down_ref[0], 1, 0).astype(BF16).T.reshape(NT, L, SW, T)
        back = dot(grad_pre, up_ref[0], 1, 1).astype(BF16).T.reshape(NT, L, SW, T)
        if joint:
            refs[3][:, 0, :L] = back
            refs[3][:, 0, L:] = down
        else:
            refs[3][:, 0, :L] = back
            refs[3][:, 0, L:] = down[:, :cut]
            refs[4][:, 0] = down[:, cut:]
        for send, ref in ((True, up_send), (False, up_keep)):
            half = rs_scr[:, 1 - core if send else core].reshape(Q * rows_up, T)
            part = scale * dot(half, grad_pre, 1, 0)
            ref[0] = part.astype(BF16).reshape(Q, rows_up, HB)
        for send, ref in ((True, down_send), (False, down_keep)):
            for q in range(Q):
                first = (2 * q + (1 - core if send else core)) * rows_down
                half = at_scr[pl.ds(pl.multiple_of(first, rows_down), rows_down)]
                ref[0, q] = (scale * dot(half, grad_mid, 1, 0)).astype(BF16)

    base = chunk * G
    widths = [2 * L] if joint else [L + cut, L - cut]
    pieces = [pltpu.HBM((NT, G, w, SW, T), BF16) for w in widths]
    piece_specs = [spec((NT, 1, w, SW, T), lambda g, s: (0, g, 0, 0, 0)) for w in widths]
    up_part = pltpu.HBM((G, Q, rows_up, HB), BF16)
    down_part = pltpu.HBM((G, Q, rows_down, BS), BF16)
    outs = pl.pallas_call(
        kernel,
        name="middle",
        grid_spec=pltpu.PrefetchScalarGridSpec(
            num_scalar_prefetch=1,
            grid=(G,),
            in_specs=[
                spec((NT, 2, 1, L, SW, T), lambda g, s: (0, 0, g, 0, 0, 0)),
                spec((1, BS, HB), lambda g, s: (base + g, 0, 0)),
                spec((1, HB, BS), lambda g, s: (base + g, 0, 0)),
            ],
            out_specs=piece_specs
            + [spec((1, Q, rows_up, HB), lambda g, s: (g, 0, 0, 0))] * 2
            + [spec((1, Q, rows_down, BS), lambda g, s: (g, 0, 0, 0))] * 2,
            scratch_shapes=[
                pltpu.VMEM((Q, 2, rows_up, T), BF16),
                pltpu.VMEM((T, HB), BF16),
                pltpu.VMEM((HB, T), BF16),
                pltpu.VMEM((T, HB), BF16),
            ],
        ),
        out_shape=pieces + [up_part] * 2 + [down_part] * 2,
        compiler_params=params(32),
        cost_estimate=LIGHT,
    )(where, *held(received, up_second, down_first))
    return outs[:-4], outs[-4:-2], outs[-2:]


def leave(where, received, places, weight, base_rows, left, scale, sizes, backward, first, count, onto=None, apart=False):
    T, L, BS, NT, G, SW, Q, _ = sizes
    rows = BS // (2 * Q)

    def kernel(where_ref, *refs):
        ins, (w_ref, base_ref, left_ref) = refs[:N_CHUNK], refs[N_CHUNK : N_CHUNK + 3]
        out_ref, low_ref, high_ref, *keeps = refs[-7 if apart else -6 : -2]
        scr, slab_scr = refs[-2:]
        core = where_ref[0]
        scr[:, 0] = ins[0][:, :, 0]
        scr[:, 1] = ins[1][:, :, 0]
        regrouped = scr[...].reshape(BS, T)
        if backward:
            branch = dot(regrouped.T, w_ref[0], 1, 1)
        else:
            branch = dot(regrouped, w_ref[0], 0, 0)
            slab_scr[...] = regrouped.reshape(Q, 2, rows, T)
        out_ref[...] = (base_ref[...].astype(F32) + branch).astype(BF16)
        for send in (True, False):
            which = 1 - core if send else core
            if backward:
                half = left_ref[0, :, which].reshape(Q * rows, T)
                part = dot(half, regrouped, 1, 1)
            else:
                half = slab_scr[:, which].reshape(Q * rows, T)
                part = dot(half, left_ref[...], 1, 0)
            part = (scale * part).astype(BF16).reshape(Q, rows, BS)
            if send:
                low_ref[0], high_ref[0] = part[:, : rows // 2], part[:, rows // 2 :]
            elif apart:
                keeps[0][0], keeps[1][0] = part[:, : rows // 2], part[:, rows // 2 :]
            else:
                keeps[0][0] = part

    cols = spec((T, BS), lambda b, s: (0, first + b))
    part = jax.ShapeDtypeStruct((count, Q, rows, BS), BF16)
    part_spec = spec((1, Q, rows, BS), lambda b, s: (b, 0, 0, 0))
    piece = jax.ShapeDtypeStruct((count, Q, rows // 2, BS), BF16)
    piece_spec = spec((1, Q, rows // 2, BS), lambda b, s: (b, 0, 0, 0))
    left_spec = spec((1, Q, 2, rows, T), lambda b, s: (first + b, 0, 0, 0, 0)) if backward else cols
    operands = held(*received, weight, base_rows, left)
    more, aliases = [], {}
    if onto is not None:
        operands += held(onto)
        more, aliases = [pl.BlockSpec(memory_space=pl.ANY)], {N_CHUNK + 4: 0}
    return pl.pallas_call(
        kernel,
        name="leave_back" if backward else "leave_out",
        grid_spec=pltpu.PrefetchScalarGridSpec(
            num_scalar_prefetch=1,
            grid=(count,),
            in_specs=[
                spec((NT, G, 1, SW, T), lambda b, s, place=place: (0, 0, place + b, 0, 0)) for place in places
            ]
            + [spec((1, BS, BS), lambda b, s: (first + b, 0, 0)), cols, left_spec]
            + more,
            out_specs=[cols, piece_spec, piece_spec] + ([piece_spec] * 2 if apart else [part_spec]),
            scratch_shapes=[
                pltpu.VMEM((NT, N_CHUNK, G, SW, T), BF16),
                pltpu.VMEM((Q, 2, rows, T), BF16),
            ],
        ),
        out_shape=[pltpu.HBM((T, L * BS), BF16), piece, piece] + ([piece] * 2 if apart else [part]),
        input_output_aliases=aliases,
        compiler_params=params(24),
        cost_estimate=LIGHT,
    )(where, *operands)


def together(*values):
    return lax.optimization_barrier(values)


def regroup(pieces, label):
    with jax.named_scope(label):
        return lax.all_to_all(pieces, "tensor", split_axis=0, concat_axis=0, tiled=True)


def swap(value, bit, label):
    count = lax.axis_size("dp")
    with jax.named_scope(label):
        return lax.ppermute(value, "dp", [(s, s ^ (1 << bit)) for s in range(count)])


def split(which, pairs, sizes):
    lead, count = sizes
    n = len(pairs)

    def kernel(which_ref, *refs):
        ins, outs = refs[: 4 * n], refs[4 * n :]
        for i in range(2 * n):
            a, b = ins[2 * i][...].astype(F32), ins[2 * i + 1][...].astype(F32)
            outs[i][...] = (a + b).astype(BF16)

    in_specs, operands, out_specs, out_shape = [], [], [], []
    for i, (keep, got, first, place) in enumerate(pairs):
        rows, width = keep.shape[2:]
        for stays in (0, 1):

            def index(a, r, which_ref, i=i, first=first, place=place, stays=stays):
                mine = which_ref[i]
                chosen = mine if stays else 1 - mine
                low = r & ((1 << place) - 1)
                return (first + a, ((r >> place) << (place + 1)) | (chosen << place) | low, 0, 0)

            in_specs += [spec((1, 1, rows, width), index)] * 2
            operands += [keep, got]
            out_specs.append(spec((1, 1, rows, width), lambda a, r, w: (a, r, 0, 0)))
            out_shape.append(pltpu.HBM((lead, count // 2, rows, width), BF16))
    outs = pl.pallas_call(
        kernel,
        name="split",
        grid_spec=pltpu.PrefetchScalarGridSpec(
            num_scalar_prefetch=1, grid=(lead, count // 2), in_specs=in_specs, out_specs=out_specs
        ),
        out_shape=out_shape,
        compiler_params=params(16),
        cost_estimate=LIGHT,
    )(which, *held(*operands))
    return [(outs[2 * i], outs[2 * i + 1]) for i in range(n)]


def whole():
    return pl.BlockSpec(memory_space=pltpu.VMEM)


def split_small(which, pairs, lead):
    n = len(pairs)
    operands = []
    for keep, got, _, _ in pairs:
        operands += [keep] + list(got)

    def kernel(which_ref, *refs):
        ins, outs = list(refs[: len(operands)]), refs[len(operands) :]
        for i, (keep, got, first, place) in enumerate(pairs):
            keep_ref, got_refs = ins.pop(0), [ins.pop(0) for _ in got]
            for stays in (0, 1):
                chosen = which_ref[i] if stays else 1 - which_ref[i]
                for r in range(keep.shape[1] // 2):
                    low = r & ((1 << place) - 1)
                    q = ((r >> place) << (place + 1)) + low + chosen * (1 << place)
                    for a in range(lead):
                        start = 0
                        for got_ref, came in zip(got_refs, got):
                            stop = start + came.shape[2]
                            total = keep_ref[first + a, q, start:stop].astype(F32) + got_ref[first + a, q].astype(F32)
                            outs[2 * i + stays][a, r, start:stop] = total.astype(BF16)
                            start = stop

    out_shape = []
    for keep, _, _, _ in pairs:
        out_shape += [jax.ShapeDtypeStruct((lead, keep.shape[1] // 2) + keep.shape[2:], BF16)] * 2
    outs = pl.pallas_call(
        kernel,
        name="small",
        in_specs=[pl.BlockSpec(memory_space=pltpu.SMEM)] + [whole()] * len(operands),
        out_specs=[whole()] * (2 * n),
        out_shape=out_shape,
        compiler_params=params(8),
        cost_estimate=LIGHT,
    )(which, *operands)
    return [(outs[2 * i], outs[2 * i + 1]) for i in range(n)]


def finish(groups):
    flat, shapes = [], []
    for pairs in groups:
        leads, rows = 0, 0
        for pair in pairs:
            halves = pair if isinstance(pair[0], tuple) else (pair,)
            leads += halves[0][0].shape[0]
            rows = sum(keep.shape[2] for keep, _ in halves)
            flat += [array for half in halves for array in half]
        shapes.append((leads, rows, flat[-1].shape[3]))

    def kernel(*refs):
        ins, outs = list(refs[: len(flat)]), refs[len(flat) :]
        for pairs, out in zip(groups, outs):
            start = 0
            for pair in pairs:
                halves = pair if isinstance(pair[0], tuple) else (pair,)
                row, leads = 0, halves[0][0].shape[0]
                for keep, _ in halves:
                    a, b = ins.pop(0), ins.pop(0)
                    rows = keep.shape[2]
                    out[start : start + leads, row : row + rows] = a[:, 0].astype(F32) + b[:, 0].astype(F32)
                    row += rows
                start += leads

    return pl.pallas_call(
        kernel,
        name="finish",
        in_specs=[whole()] * len(flat),
        out_shape=[jax.ShapeDtypeStruct(shape, F32) for shape in shapes],
        compiler_params=params(16),
        cost_estimate=LIGHT,
    )(*flat)


class Halving:
    def __init__(self, streams, label, large, turned=0):
        self.label = label
        self.large = large
        self.bits = bits = (lax.axis_size("dp") // 2).bit_length() - 1
        self.orders = [list(range(bits))[:: -1 if (i + turned) % 2 else 1] for i in range(len(streams))]
        self.held = [list(range(bits)) for _ in streams]
        self.streams = streams

    def add(self, lead):
        index = lax.axis_index("dp")
        pairs, mine = [], []
        self.moving = []
        for (keep, got, first), order, held in zip(self.streams, self.orders, self.held):
            bit = order.pop(0)
            pairs.append((keep, got, first, held.index(bit)))
            held.remove(bit)
            mine.append((index >> (bit + 1)) & 1)
            self.moving.append(bit)
        which = jnp.stack(mine).astype(jnp.int32)
        if self.large and len(self.held[0]) == self.bits - 1:
            pairs = [(keep, got[0], first, place) for keep, got, first, place in pairs]
            self.parts = split(which, pairs, (lead, pairs[0][0].shape[1]))
        else:
            self.parts = split_small(which, pairs, lead)
        return [outgoing for outgoing, _ in self.parts]

    def move(self, outgoing):
        self.streams = [
            (staying, [swap(out, bit + 1, "%s_bit%d" % (self.label, bit))], 0)
            for out, (_, staying), bit in zip(outgoing, self.parts, self.moving)
        ]

    def got(self):
        return [array for _, got, _ in self.streams for array in got]

    def replace(self, arrived):
        arrived = list(arrived)
        self.streams = [
            (keep, [arrived.pop(0) for _ in got], first) for keep, got, first in self.streams
        ]

    def run(self, lead):
        while self.orders[0]:
            self.move(self.add(lead))
        return [(keep, got[0]) for keep, got, _ in self.streams]


def body(tokens, up_first, up_second, down_first, down_second, cotangent):
    T = tokens.shape[0]
    L, BS = up_first.shape[0], up_first.shape[1]
    HB = up_second.shape[2]
    NT = lax.axis_size("tensor")
    n_dp = lax.axis_size("dp")
    scale = (T * n_dp) ** (-0.5)
    sizes = (T, L, BS, NT, L // N_CHUNK, BS // NB, n_dp // 2, HB)
    where = (lax.axis_index("dp") % 2).astype(jnp.int32).reshape(1)

    lead = L // N_CHUNK
    half = L // 2
    cut = max(L // 4, 1)

    def middle_sums(parts, label, before):
        (up_send, up_keep), (down_send, down_keep) = parts
        if before is not None:
            up_send, down_send, *got = together(up_send, down_send, *before.got())
            before.replace(got)
        got_up, got_down = swap(up_send, 0, label + "_core"), swap(down_send, 0, label + "_core")
        return Halving([(up_keep, [got_up], 0), (down_keep, [got_down], 0)], label, True)

    first_0, first_1 = enter(tokens, up_first, cotangent, down_second, sizes)
    in_0 = regroup(first_0, "z1")
    x_turned = turn(tokens, sizes)
    in_0, first_1, x_turned = together(in_0, first_1, x_turned)
    in_1 = regroup(first_1, "z2")
    (both_0,), *parts = middle(where, in_0, up_second, down_first, 0, scale, sizes, True)
    mid_0 = middle_sums(parts, "mid0", None)
    leaving_0 = mid_0.add(lead)
    in_1, both_0, *_ = together(in_1, both_0, *leaving_0)
    both_0 = regroup(both_0, "z3")
    mid_0.move(leaving_0)
    (most_1, rest_1), *parts = middle(where, in_1, up_second, down_first, 1, scale, sizes, False)
    mid_1 = middle_sums(parts, "mid1", mid_0)
    leaving_0 = mid_0.add(lead)
    both_0, most_1, *_ = together(both_0, most_1, *leaving_0)
    most_1 = regroup(most_1, "z4")
    mid_0.move(leaving_0)
    leaving_1 = mid_1.add(lead)
    got = together(*mid_0.got(), *leaving_1)
    mid_0.replace(got[:2])
    leaving_1 = got[2:]
    mid_1.move(leaving_1)
    most_1, rest_1, *_ = together(most_1, rest_1, *leaving_1)
    rest_1 = regroup(rest_1, "z5")
    grad_tokens, parts = None, []
    for start, count in ((0, half), (half, L - half)):
        grad_tokens, *part = leave(
            where,
            (both_0, most_1),
            (start, start),
            up_first,
            cotangent,
            x_turned,
            scale,
            sizes,
            True,
            start,
            count,
            grad_tokens,
        )
        parts.append(part)
    def edge_sums(halves, label, turned):
        streams = [(part[2], [swap(piece, 0, label + "_core") for piece in part[:2]], 0) for part in halves]
        return Halving(streams, label, False, turned)

    edge_first = edge_sums(parts, "first", 0)
    layer_out, *low = leave(
        where, (both_0, most_1), (L, L), down_second, tokens, cotangent, scale, sizes, False, 0, cut
    )
    edge_low = edge_sums([low], "low", 0)
    leaving_first = edge_first.add(lead)
    leaving_low = edge_low.add(cut)
    leaving_1 = mid_1.add(lead) if mid_1.orders[0] else []
    edge_first.move(leaving_first)
    edge_low.move(leaving_low)
    mid_1.move(leaving_1)
    rest_1, *_ = together(rest_1, *leaving_first, *leaving_low, *leaving_1)
    layer_out, *high = leave(
        where,
        (both_0, rest_1),
        (L + cut, 0),
        down_second,
        tokens,
        cotangent,
        scale,
        sizes,
        False,
        cut,
        L - cut,
        layer_out,
        True,
    )
    waited = (mid_1,)
    high[0], high[1], *got = together(*high[:2], *[array for sums in waited for array in sums.got()])
    for sums in waited:
        count = len(sums.got())
        sums.replace(got[:count])
        got = got[count:]
    streams = [(keep, [swap(send, 0, "high_core")], 0) for send, keep in zip(high[:2], high[2:])]
    edge_high = Halving(streams, "high", False)
    edge_high.move(edge_high.add(L - cut))
    done_0, done_1 = mid_0.run(lead), mid_1.run(lead)
    grad_up_second, grad_down_first = finish([[done_0[0], done_1[0]], [done_0[1], done_1[1]]])
    done_first, done_low = edge_first.run(lead), edge_low.run(cut)
    got = together(*edge_high.got(), grad_up_second, grad_down_first)
    edge_high.replace(got[:-2])
    done_high = edge_high.run(L - cut)
    (grad_up_first,) = finish([done_first])
    (grad_down_second,) = finish([done_low + [tuple(done_high)]])
    return (
        layer_out,
        grad_tokens,
        grad_up_first.reshape(L, -1, BS),
        got[-2].reshape(L, -1, HB),
        got[-1].reshape(L, -1, BS),
        grad_down_second.reshape(L, -1, BS),
    )


def solution(mesh):
    in_specs = (
        P("dp", "tensor"),
        P("tensor", None, None),
        P("tensor", None, None),
        P("tensor", None, None),
        P("tensor", None, None),
        P("dp", "tensor"),
    )
    out_specs = (
        P("dp", "tensor"),
        P("dp", "tensor"),
        P("tensor", "dp", None),
        P("tensor", "dp", None),
        P("tensor", "dp", None),
        P("tensor", "dp", None),
    )
    return jax.shard_map(body, mesh=mesh, in_specs=in_specs, out_specs=out_specs, check_vma=False)
```

```python
import jax
import jax.numpy as jnp
from jax import lax
from jax.experimental import pallas as pl
from jax.experimental.pallas import tpu as pltpu
from jax.sharding import PartitionSpec as P

NB = 16
N_CHUNK = 2

gelu_coeff = 0.7978845608028654
cubic_coeff = 0.044715

BF16 = jnp.bfloat16
F32 = jnp.float32


def gelu_pair(hidden):
    inner_arg = gelu_coeff * (hidden + cubic_coeff * hidden * hidden * hidden)
    tangent = jnp.tanh(inner_arg)
    gelu_value = 0.5 * hidden * (1.0 + tangent)
    gelu_slope = 0.5 * (1.0 + tangent) + 0.5 * hidden * (1.0 - tangent * tangent) * gelu_coeff * (
        1.0 + 3.0 * cubic_coeff * hidden * hidden
    )
    return gelu_value, gelu_slope


def dot(a, b, ca, cb):
    return lax.dot_general(a, b, (((ca,), (cb,)), ((), ())), preferred_element_type=F32)


def params(mebibytes):
    return pltpu.CompilerParams(vmem_limit_bytes=mebibytes * 1024 * 1024)


def held(*values):
    return [pltpu.with_memory_space_constraint(v, pltpu.HBM) for v in values]


def spec(block, index_map):
    return pl.BlockSpec(block, index_map)


LIGHT = pl.CostEstimate(flops=0, transcendentals=0, bytes_accessed=0)


def enter(tokens, up_first, cotangent, down_second, sizes):
    T, L, BS, NT, G, SW, Q, _ = sizes

    def kernel(x_ref, w_ref, g_ref, d_ref, *outs):
        up = dot(x_ref[...], w_ref[0], 1, 0).astype(BF16).T.reshape(NT, L, SW, T)
        back = dot(d_ref[0], g_ref[...], 1, 1).astype(BF16).reshape(NT, L, SW, T)
        for chunk in range(N_CHUNK):
            outs[chunk][:, 0, :, 0] = up[:, chunk * G : (chunk + 1) * G]
            outs[chunk][:, 1, :, 0] = back[:, chunk * G : (chunk + 1) * G]

    cols = spec((T, BS), lambda b: (0, b))
    square = spec((1, BS, BS), lambda b: (b, 0, 0))
    outs = pl.pallas_call(
        kernel,
        name="enter",
        grid=(L,),
        in_specs=[cols, square, cols, square],
        out_specs=[spec((NT, 2, G, 1, SW, T), lambda b: (0, 0, 0, b, 0, 0))] * N_CHUNK,
        out_shape=[pltpu.HBM((NT, 2, G, L, SW, T), BF16)] * N_CHUNK,
        compiler_params=params(56),
        cost_estimate=LIGHT,
    )(*held(tokens, up_first, cotangent, down_second))
    return outs


def turn(tokens, sizes):
    T, L, BS, _, _, _, Q, _ = sizes
    rows = BS // (2 * Q)

    def kernel(x_ref, out_ref):
        out_ref[0] = x_ref[...].T.reshape(Q, 2, rows, T)

    return pl.pallas_call(
        kernel,
        name="turn",
        grid=(L,),
        in_specs=[spec((T, BS), lambda b: (0, b))],
        out_specs=spec((1, Q, 2, rows, T), lambda b: (b, 0, 0, 0, 0)),
        out_shape=pltpu.HBM((L, Q, 2, rows, T), BF16),
        compiler_params=params(56),
        cost_estimate=LIGHT,
    )(*held(tokens))


def middle(where, received, up_second, down_first, chunk, scale, sizes, joint):
    T, L, BS, NT, G, SW, Q, HB = sizes
    rows_up, rows_down = BS // (2 * Q), HB // (2 * Q)
    cut = max(L // 4, 1)
    tile = min(512, HB)

    def kernel(where_ref, *refs):
        in_ref, up_ref, down_ref = refs[:3]
        up_send, up_keep, down_send, down_keep, rs_scr, act_scr, at_scr, gp_scr = refs[-8:]
        core = where_ref[0]
        regrouped = in_ref[:, 0, 0].reshape(BS, T)
        rs_scr[...] = regrouped.reshape(Q, 2, rows_up, T)
        turned = regrouped.T
        grad_mid = in_ref[:, 1, 0].reshape(BS, T).T
        for start in range(0, HB, tile):
            pre = dot(turned, up_ref[0, :, start : start + tile], 1, 0)
            value, slope = gelu_pair(pre)
            value = value.astype(BF16)
            act_scr[:, start : start + tile] = value
            at_scr[start : start + tile] = value.T
            grad_act = dot(grad_mid, down_ref[0, start : start + tile], 1, 1)
            gp_scr[:, start : start + tile] = (grad_act * slope).astype(BF16)
        activated = act_scr[...]
        grad_pre = gp_scr[...]
        down = dot(activated, down_ref[0], 1, 0).astype(BF16).T.reshape(NT, L, SW, T)
        back = dot(grad_pre, up_ref[0], 1, 1).astype(BF16).T.reshape(NT, L, SW, T)
        if joint:
            refs[3][:, 0, :L] = back
            refs[3][:, 0, L:] = down
        else:
            refs[3][:, 0, :L] = back
            refs[3][:, 0, L:] = down[:, :cut]
            refs[4][:, 0] = down[:, cut:]
        for send, ref in ((True, up_send), (False, up_keep)):
            half = rs_scr[:, 1 - core if send else core].reshape(Q * rows_up, T)
            part = scale * dot(half, grad_pre, 1, 0)
            ref[0] = part.astype(BF16).reshape(Q, rows_up, HB)
        for send, ref in ((True, down_send), (False, down_keep)):
            for q in range(Q):
                first = (2 * q + (1 - core if send else core)) * rows_down
                half = at_scr[pl.ds(pl.multiple_of(first, rows_down), rows_down)]
                ref[0, q] = (scale * dot(half, grad_mid, 1, 0)).astype(BF16)

    base = chunk * G
    widths = [2 * L] if joint else [L + cut, L - cut]
    pieces = [pltpu.HBM((NT, G, w, SW, T), BF16) for w in widths]
    piece_specs = [spec((NT, 1, w, SW, T), lambda g, s: (0, g, 0, 0, 0)) for w in widths]
    up_part = pltpu.HBM((G, Q, rows_up, HB), BF16)
    down_part = pltpu.HBM((G, Q, rows_down, BS), BF16)
    outs = pl.pallas_call(
        kernel,
        name="middle",
        grid_spec=pltpu.PrefetchScalarGridSpec(
            num_scalar_prefetch=1,
            grid=(G,),
            in_specs=[
                spec((NT, 2, 1, L, SW, T), lambda g, s: (0, 0, g, 0, 0, 0)),
                spec((1, BS, HB), lambda g, s: (base + g, 0, 0)),
                spec((1, HB, BS), lambda g, s: (base + g, 0, 0)),
            ],
            out_specs=piece_specs
            + [spec((1, Q, rows_up, HB), lambda g, s: (g, 0, 0, 0))] * 2
            + [spec((1, Q, rows_down, BS), lambda g, s: (g, 0, 0, 0))] * 2,
            scratch_shapes=[
                pltpu.VMEM((Q, 2, rows_up, T), BF16),
                pltpu.VMEM((T, HB), BF16),
                pltpu.VMEM((HB, T), BF16),
                pltpu.VMEM((T, HB), BF16),
            ],
        ),
        out_shape=pieces + [up_part] * 2 + [down_part] * 2,
        compiler_params=params(32),
        cost_estimate=LIGHT,
    )(where, *held(received, up_second, down_first))
    return outs[:-4], outs[-4:-2], outs[-2:]


def leave(where, received, places, weight, base_rows, left, scale, sizes, backward, first, count, onto=None, cut=None):
    T, L, BS, NT, G, SW, Q, _ = sizes
    rows = BS // (2 * Q)
    n_in = len(places)

    def kernel(where_ref, *refs):
        ins, (w_ref, base_ref, left_ref) = refs[:n_in], refs[n_in : n_in + 3]
        out_ref, low_ref, high_ref, low_keep, high_keep, scr, slab_scr = refs[-7:]
        core = where_ref[0]
        scr[:, 0] = ins[0][:, :, 0]
        if cut is not None:

            @pl.when(pl.program_id(0) < cut)
            def _():
                scr[:, 1] = ins[1][:, :, 0]

            @pl.when(pl.program_id(0) >= cut)
            def _():
                scr[:, 1] = ins[2][:, :, 0]
        else:
            scr[:, 1] = ins[1][:, :, 0]
        regrouped = scr[...].reshape(BS, T)
        if backward:
            branch = dot(regrouped.T, w_ref[0], 1, 1)
        else:
            branch = dot(regrouped, w_ref[0], 0, 0)
            slab_scr[...] = regrouped.reshape(Q, 2, rows, T)
        out_ref[...] = (base_ref[...].astype(F32) + branch).astype(BF16)
        for send in (True, False):
            which = 1 - core if send else core
            if backward:
                half = left_ref[0, :, which].reshape(Q * rows, T)
                part = dot(half, regrouped, 1, 1)
            else:
                half = slab_scr[:, which].reshape(Q * rows, T)
                part = dot(half, left_ref[...], 1, 0)
            part = (scale * part).astype(BF16).reshape(Q, rows, BS)
            if send:
                low_ref[0], high_ref[0] = part[:, : rows // 2], part[:, rows // 2 :]
            else:
                low_keep[0], high_keep[0] = part[:, : rows // 2], part[:, rows // 2 :]

    cols = spec((T, BS), lambda b, s: (0, first + b))
    piece = jax.ShapeDtypeStruct((count, Q, rows // 2, BS), BF16)
    piece_spec = spec((1, Q, rows // 2, BS), lambda b, s: (b, 0, 0, 0))
    left_spec = spec((1, Q, 2, rows, T), lambda b, s: (first + b, 0, 0, 0, 0)) if backward else cols
    operands = held(*received, weight, base_rows, left)
    more, aliases = [], {}
    if onto is not None:
        operands += held(onto)
        more, aliases = [pl.BlockSpec(memory_space=pl.ANY)], {n_in + 4: 0}
    return pl.pallas_call(
        kernel,
        name="leave_back" if backward else "leave_out",
        grid_spec=pltpu.PrefetchScalarGridSpec(
            num_scalar_prefetch=1,
            grid=(count,),
            in_specs=[
                spec((NT, G, 1, SW, T), lambda b, s, place=place: (0, 0, place(b), 0, 0)) for place in places
            ]
            + [spec((1, BS, BS), lambda b, s: (first + b, 0, 0)), cols, left_spec]
            + more,
            out_specs=[cols] + [piece_spec] * 4,
            scratch_shapes=[
                pltpu.VMEM((NT, N_CHUNK, G, SW, T), BF16),
                pltpu.VMEM((Q, 2, rows, T), BF16),
            ],
        ),
        out_shape=[pltpu.HBM((T, L * BS), BF16)] + [piece] * 4,
        input_output_aliases=aliases,
        compiler_params=params(24),
        cost_estimate=LIGHT,
    )(where, *operands)


def together(*values):
    return lax.optimization_barrier(values)


def regroup(pieces, label):
    with jax.named_scope(label):
        return lax.all_to_all(pieces, "tensor", split_axis=0, concat_axis=0, tiled=True)


def swap(value, bit, label):
    count = lax.axis_size("dp")
    with jax.named_scope(label):
        return lax.ppermute(value, "dp", [(s, s ^ (1 << bit)) for s in range(count)])


def split(which, pairs, sizes):
    lead, count = sizes
    n = len(pairs)

    def kernel(which_ref, *refs):
        ins, outs = refs[: 4 * n], refs[4 * n :]
        for i in range(2 * n):
            a, b = ins[2 * i][...].astype(F32), ins[2 * i + 1][...].astype(F32)
            outs[i][...] = (a + b).astype(BF16)

    in_specs, operands, out_specs, out_shape = [], [], [], []
    for i, (keep, got, first, place) in enumerate(pairs):
        rows, width = keep.shape[2:]
        for stays in (0, 1):

            def index(a, r, which_ref, i=i, first=first, place=place, stays=stays):
                mine = which_ref[i]
                chosen = mine if stays else 1 - mine
                low = r & ((1 << place) - 1)
                return (first + a, ((r >> place) << (place + 1)) | (chosen << place) | low, 0, 0)

            in_specs += [spec((1, 1, rows, width), index)] * 2
            operands += [keep, got]
            out_specs.append(spec((1, 1, rows, width), lambda a, r, w: (a, r, 0, 0)))
            out_shape.append(pltpu.HBM((lead, count // 2, rows, width), BF16))
    outs = pl.pallas_call(
        kernel,
        name="split",
        grid_spec=pltpu.PrefetchScalarGridSpec(
            num_scalar_prefetch=1, grid=(lead, count // 2), in_specs=in_specs, out_specs=out_specs
        ),
        out_shape=out_shape,
        compiler_params=params(16),
        cost_estimate=LIGHT,
    )(which, *held(*operands))
    return [(outs[2 * i], outs[2 * i + 1]) for i in range(n)]


def whole():
    return pl.BlockSpec(memory_space=pltpu.VMEM)


def split_small(which, pairs, lead):
    n = len(pairs)
    operands = []
    for keep, got, _, _ in pairs:
        operands += [keep] + list(got)

    def kernel(which_ref, *refs):
        ins, outs = list(refs[: len(operands)]), refs[len(operands) :]
        for i, (keep, got, first, place) in enumerate(pairs):
            keep_ref, got_refs = ins.pop(0), [ins.pop(0) for _ in got]
            for stays in (0, 1):
                chosen = which_ref[i] if stays else 1 - which_ref[i]
                for r in range(keep.shape[1] // 2):
                    low = r & ((1 << place) - 1)
                    q = ((r >> place) << (place + 1)) + low + chosen * (1 << place)
                    for a in range(lead):
                        start = 0
                        for got_ref, came in zip(got_refs, got):
                            stop = start + came.shape[2]
                            total = keep_ref[first + a, q, start:stop].astype(F32) + got_ref[first + a, q].astype(F32)
                            outs[2 * i + stays][a, r, start:stop] = total.astype(BF16)
                            start = stop

    out_shape = []
    for keep, _, _, _ in pairs:
        out_shape += [jax.ShapeDtypeStruct((lead, keep.shape[1] // 2) + keep.shape[2:], BF16)] * 2
    outs = pl.pallas_call(
        kernel,
        name="small",
        in_specs=[pl.BlockSpec(memory_space=pltpu.SMEM)] + [whole()] * len(operands),
        out_specs=[whole()] * (2 * n),
        out_shape=out_shape,
        compiler_params=params(8),
        cost_estimate=LIGHT,
    )(which, *operands)
    return [(outs[2 * i], outs[2 * i + 1]) for i in range(n)]


def finish(groups):
    flat, shapes = [], []
    for pairs in groups:
        leads, rows = 0, 0
        for pair in pairs:
            halves = pair if isinstance(pair[0], tuple) else (pair,)
            leads += halves[0][0].shape[0]
            rows = sum(keep.shape[2] for keep, _ in halves)
            flat += [array for half in halves for array in half]
        shapes.append((leads, rows, flat[-1].shape[3]))

    def kernel(*refs):
        ins, outs = list(refs[: len(flat)]), refs[len(flat) :]
        for pairs, out in zip(groups, outs):
            start = 0
            for pair in pairs:
                halves = pair if isinstance(pair[0], tuple) else (pair,)
                row, leads = 0, halves[0][0].shape[0]
                for keep, _ in halves:
                    a, b = ins.pop(0), ins.pop(0)
                    rows = keep.shape[2]
                    out[start : start + leads, row : row + rows] = a[:, 0].astype(F32) + b[:, 0].astype(F32)
                    row += rows
                start += leads

    return pl.pallas_call(
        kernel,
        name="finish",
        in_specs=[whole()] * len(flat),
        out_shape=[jax.ShapeDtypeStruct(shape, F32) for shape in shapes],
        compiler_params=params(16),
        cost_estimate=LIGHT,
    )(*flat)


class Halving:
    def __init__(self, streams, label, large, turned=0):
        self.label = label
        self.large = large
        self.bits = bits = (lax.axis_size("dp") // 2).bit_length() - 1
        self.orders = [list(range(bits))[:: -1 if (i + turned) % 2 else 1] for i in range(len(streams))]
        self.held = [list(range(bits)) for _ in streams]
        self.streams = streams

    def add(self, lead):
        index = lax.axis_index("dp")
        pairs, mine = [], []
        self.moving = []
        for (keep, got, first), order, held in zip(self.streams, self.orders, self.held):
            bit = order.pop(0)
            pairs.append((keep, got, first, held.index(bit)))
            held.remove(bit)
            mine.append((index >> (bit + 1)) & 1)
            self.moving.append(bit)
        which = jnp.stack(mine).astype(jnp.int32)
        if self.large and len(self.held[0]) == self.bits - 1:
            pairs = [(keep, got[0], first, place) for keep, got, first, place in pairs]
            self.parts = split(which, pairs, (lead, pairs[0][0].shape[1]))
        else:
            self.parts = split_small(which, pairs, lead)
        return [outgoing for outgoing, _ in self.parts]

    def move(self, outgoing):
        self.streams = [
            (staying, [swap(out, bit + 1, "%s_bit%d" % (self.label, bit))], 0)
            for out, (_, staying), bit in zip(outgoing, self.parts, self.moving)
        ]

    def got(self):
        return [array for _, got, _ in self.streams for array in got]

    def replace(self, arrived):
        arrived = list(arrived)
        self.streams = [
            (keep, [arrived.pop(0) for _ in got], first) for keep, got, first in self.streams
        ]

    def run(self, lead):
        while self.orders[0]:
            self.move(self.add(lead))
        return [(keep, got[0]) for keep, got, _ in self.streams]


def body(tokens, up_first, up_second, down_first, down_second, cotangent):
    T = tokens.shape[0]
    L, BS = up_first.shape[0], up_first.shape[1]
    HB = up_second.shape[2]
    NT = lax.axis_size("tensor")
    n_dp = lax.axis_size("dp")
    scale = (T * n_dp) ** (-0.5)
    sizes = (T, L, BS, NT, L // N_CHUNK, BS // NB, n_dp // 2, HB)
    where = (lax.axis_index("dp") % 2).astype(jnp.int32).reshape(1)

    lead = L // N_CHUNK
    half = L // 2
    cut = max(L // 4, 1)

    def middle_sums(parts, label, before):
        (up_send, up_keep), (down_send, down_keep) = parts
        if before is not None:
            up_send, down_send, *got = together(up_send, down_send, *before.got())
            before.replace(got)
        got_up, got_down = swap(up_send, 0, label + "_core"), swap(down_send, 0, label + "_core")
        return Halving([(up_keep, [got_up], 0), (down_keep, [got_down], 0)], label, True)

    first_0, first_1 = enter(tokens, up_first, cotangent, down_second, sizes)
    in_0 = regroup(first_0, "z1")
    x_turned = turn(tokens, sizes)
    in_0, first_1, x_turned = together(in_0, first_1, x_turned)
    in_1 = regroup(first_1, "z2")
    (both_0,), *parts = middle(where, in_0, up_second, down_first, 0, scale, sizes, True)
    mid_0 = middle_sums(parts, "mid0", None)
    leaving_0 = mid_0.add(lead)
    in_1, both_0, *_ = together(in_1, both_0, *leaving_0)
    both_0 = regroup(both_0, "z3")
    mid_0.move(leaving_0)
    (most_1, rest_1), *parts = middle(where, in_1, up_second, down_first, 1, scale, sizes, False)
    mid_1 = middle_sums(parts, "mid1", mid_0)
    leaving_0 = mid_0.add(lead)
    both_0, most_1, *_ = together(both_0, most_1, *leaving_0)
    most_1 = regroup(most_1, "z4")
    mid_0.move(leaving_0)
    leaving_1 = mid_1.add(lead)
    got = together(*mid_0.got(), *leaving_1)
    mid_0.replace(got[:2])
    leaving_1 = got[2:]
    mid_1.move(leaving_1)
    most_1, rest_1, *_ = together(most_1, rest_1, *leaving_1)
    rest_1 = regroup(rest_1, "z5")
    def edge_sums(halves, label):
        streams = [(keep, [swap(out, 0, label + "_core")], 0) for out, keep in zip(halves[:2], halves[2:])]
        return Halving(streams, label, False)

    grad_tokens, *first = leave(
        where, (both_0, most_1), [lambda b: b] * 2, up_first, cotangent, x_turned, scale, sizes, True, 0, L
    )
    edge_first = edge_sums(first, "first")
    leaving_first = edge_first.add(L)
    leaving_1 = mid_1.add(lead) if mid_1.orders[0] else []
    edge_first.move(leaving_first)
    mid_1.move(leaving_1)
    rest_1, *_ = together(rest_1, *leaving_first, *leaving_1)
    layer_out, *high = leave(
        where,
        (both_0, most_1, rest_1),
        [lambda b: L + b, lambda b: L + jnp.minimum(b, cut - 1), lambda b: jnp.maximum(b - cut, 0)],
        down_second,
        tokens,
        cotangent,
        scale,
        sizes,
        False,
        0,
        L,
        None,
        cut,
    )
    waited = (mid_1,)
    high[0], high[1], *got = together(*high[:2], *[array for sums in waited for array in sums.got()])
    for sums in waited:
        count = len(sums.got())
        sums.replace(got[:count])
        got = got[count:]
    edge_high = edge_sums(high, "high")
    edge_high.move(edge_high.add(L))
    done_0, done_1 = mid_0.run(lead), mid_1.run(lead)
    grad_up_second, grad_down_first = finish([[done_0[0], done_1[0]], [done_0[1], done_1[1]]])
    done_first = edge_first.run(L)
    got = together(*edge_high.got(), grad_up_second, grad_down_first)
    edge_high.replace(got[:-2])
    done_high = edge_high.run(L)
    (grad_up_first,) = finish([[tuple(done_first)]])
    (grad_down_second,) = finish([[tuple(done_high)]])
    return (
        layer_out,
        grad_tokens,
        grad_up_first.reshape(L, -1, BS),
        got[-2].reshape(L, -1, HB),
        got[-1].reshape(L, -1, BS),
        grad_down_second.reshape(L, -1, BS),
    )


def solution(mesh):
    in_specs = (
        P("dp", "tensor"),
        P("tensor", None, None),
        P("tensor", None, None),
        P("tensor", None, None),
        P("tensor", None, None),
        P("dp", "tensor"),
    )
    out_specs = (
        P("dp", "tensor"),
        P("dp", "tensor"),
        P("tensor", "dp", None),
        P("tensor", "dp", None),
        P("tensor", "dp", None),
        P("tensor", "dp", None),
    )
    return jax.shard_map(body, mesh=mesh, in_specs=in_specs, out_specs=out_specs, check_vma=False)
```

```python
import jax
import jax.numpy as jnp
from jax import lax
from jax.experimental import pallas as pl
from jax.experimental.pallas import tpu as pltpu
from jax.sharding import PartitionSpec as P

NB = 16
N_CHUNK = 2

gelu_coeff = 0.7978845608028654
cubic_coeff = 0.044715

BF16 = jnp.bfloat16
F32 = jnp.float32


def gelu_pair(hidden):
    inner_arg = gelu_coeff * (hidden + cubic_coeff * hidden * hidden * hidden)
    tangent = jnp.tanh(inner_arg)
    gelu_value = 0.5 * hidden * (1.0 + tangent)
    gelu_slope = 0.5 * (1.0 + tangent) + 0.5 * hidden * (1.0 - tangent * tangent) * gelu_coeff * (
        1.0 + 3.0 * cubic_coeff * hidden * hidden
    )
    return gelu_value, gelu_slope


def dot(a, b, ca, cb):
    return lax.dot_general(a, b, (((ca,), (cb,)), ((), ())), preferred_element_type=F32)


def params(mebibytes):
    return pltpu.CompilerParams(vmem_limit_bytes=mebibytes * 1024 * 1024)


def held(*values):
    return [pltpu.with_memory_space_constraint(v, pltpu.HBM) for v in values]


def spec(block, index_map):
    return pl.BlockSpec(block, index_map)


LIGHT = pl.CostEstimate(flops=0, transcendentals=0, bytes_accessed=0)


def enter(tokens, up_first, cotangent, down_second, sizes):
    T, L, BS, NT, G, SW, Q, _ = sizes

    def kernel(x_ref, w_ref, g_ref, d_ref, *outs):
        up = dot(x_ref[...], w_ref[0], 1, 0).astype(BF16).T.reshape(NT, L, SW, T)
        back = dot(d_ref[0], g_ref[...], 1, 1).astype(BF16).reshape(NT, L, SW, T)
        for chunk in range(N_CHUNK):
            outs[chunk][:, 0, :, 0] = up[:, chunk * G : (chunk + 1) * G]
            outs[chunk][:, 1, :, 0] = back[:, chunk * G : (chunk + 1) * G]

    cols = spec((T, BS), lambda b: (0, b))
    square = spec((1, BS, BS), lambda b: (b, 0, 0))
    outs = pl.pallas_call(
        kernel,
        name="enter",
        grid=(L,),
        in_specs=[cols, square, cols, square],
        out_specs=[spec((NT, 2, G, 1, SW, T), lambda b: (0, 0, 0, b, 0, 0))] * N_CHUNK,
        out_shape=[pltpu.HBM((NT, 2, G, L, SW, T), BF16)] * N_CHUNK,
        compiler_params=params(56),
        cost_estimate=LIGHT,
    )(*held(tokens, up_first, cotangent, down_second))
    return outs


def turn(tokens, sizes):
    T, L, BS, _, _, _, Q, _ = sizes
    rows = BS // (2 * Q)

    def kernel(x_ref, out_ref):
        out_ref[0] = x_ref[...].T.reshape(Q, 2, rows, T)

    return pl.pallas_call(
        kernel,
        name="turn",
        grid=(L,),
        in_specs=[spec((T, BS), lambda b: (0, b))],
        out_specs=spec((1, Q, 2, rows, T), lambda b: (b, 0, 0, 0, 0)),
        out_shape=pltpu.HBM((L, Q, 2, rows, T), BF16),
        compiler_params=params(56),
        cost_estimate=LIGHT,
    )(*held(tokens))


def middle(where, received, up_second, down_first, chunk, scale, sizes, joint):
    T, L, BS, NT, G, SW, Q, HB = sizes
    rows_up, rows_down = BS // (2 * Q), HB // (2 * Q)
    cut = max(L // 4, 1)
    tile = min(512, HB)

    def kernel(where_ref, *refs):
        in_ref, up_ref, down_ref = refs[:3]
        up_send, up_keep, down_send, down_keep, rs_scr, act_scr, at_scr, gp_scr = refs[-8:]
        core = where_ref[0]
        regrouped = in_ref[:, 0, 0].reshape(BS, T)
        rs_scr[...] = regrouped.reshape(Q, 2, rows_up, T)
        turned = regrouped.T
        grad_mid = in_ref[:, 1, 0].reshape(BS, T).T
        for start in range(0, HB, tile):
            pre = dot(turned, up_ref[0, :, start : start + tile], 1, 0)
            value, slope = gelu_pair(pre)
            value = value.astype(BF16)
            act_scr[:, start : start + tile] = value
            at_scr[start : start + tile] = value.T
            grad_act = dot(grad_mid, down_ref[0, start : start + tile], 1, 1)
            gp_scr[:, start : start + tile] = (grad_act * slope).astype(BF16)
        activated = act_scr[...]
        grad_pre = gp_scr[...]
        down = dot(activated, down_ref[0], 1, 0).astype(BF16).T.reshape(NT, L, SW, T)
        back = dot(grad_pre, up_ref[0], 1, 1).astype(BF16).T.reshape(NT, L, SW, T)
        if joint:
            refs[3][:, 0, :L] = back
            refs[3][:, 0, L:] = down
        else:
            refs[3][:, 0, :L] = back
            refs[3][:, 0, L:] = down[:, :cut]
            refs[4][:, 0] = down[:, cut:]
        for send, ref in ((True, up_send), (False, up_keep)):
            half = rs_scr[:, 1 - core if send else core].reshape(Q * rows_up, T)
            part = scale * dot(half, grad_pre, 1, 0)
            ref[0] = part.astype(BF16).reshape(Q, rows_up, HB)
        for send, ref in ((True, down_send), (False, down_keep)):
            for q in range(Q):
                first = (2 * q + (1 - core if send else core)) * rows_down
                half = at_scr[pl.ds(pl.multiple_of(first, rows_down), rows_down)]
                ref[0, q] = (scale * dot(half, grad_mid, 1, 0)).astype(BF16)

    base = chunk * G
    widths = [2 * L] if joint else [L + cut, L - cut]
    pieces = [pltpu.HBM((NT, G, w, SW, T), BF16) for w in widths]
    piece_specs = [spec((NT, 1, w, SW, T), lambda g, s: (0, g, 0, 0, 0)) for w in widths]
    up_part = pltpu.HBM((G, Q, rows_up, HB), BF16)
    down_part = pltpu.HBM((G, Q, rows_down, BS), BF16)
    outs = pl.pallas_call(
        kernel,
        name="middle",
        grid_spec=pltpu.PrefetchScalarGridSpec(
            num_scalar_prefetch=1,
            grid=(G,),
            in_specs=[
                spec((NT, 2, 1, L, SW, T), lambda g, s: (0, 0, g, 0, 0, 0)),
                spec((1, BS, HB), lambda g, s: (base + g, 0, 0)),
                spec((1, HB, BS), lambda g, s: (base + g, 0, 0)),
            ],
            out_specs=piece_specs
            + [spec((1, Q, rows_up, HB), lambda g, s: (g, 0, 0, 0))] * 2
            + [spec((1, Q, rows_down, BS), lambda g, s: (g, 0, 0, 0))] * 2,
            scratch_shapes=[
                pltpu.VMEM((Q, 2, rows_up, T), BF16),
                pltpu.VMEM((T, HB), BF16),
                pltpu.VMEM((HB, T), BF16),
                pltpu.VMEM((T, HB), BF16),
            ],
        ),
        out_shape=pieces + [up_part] * 2 + [down_part] * 2,
        compiler_params=params(32),
        cost_estimate=LIGHT,
    )(where, *held(received, up_second, down_first))
    return outs[:-4], outs[-4:-2], outs[-2:]


def leave(where, received, places, weight, base_rows, left, scale, sizes, backward, first, count, onto=None, cut=None):
    T, L, BS, NT, G, SW, Q, _ = sizes
    rows = BS // (2 * Q)
    n_in = len(places)

    def kernel(where_ref, *refs):
        ins, (w_ref, base_ref, left_ref) = refs[:n_in], refs[n_in : n_in + 3]
        out_ref, low_ref, high_ref, low_keep, high_keep, scr, slab_scr = refs[-7:]
        core = where_ref[0]
        scr[:, 0] = ins[0][:, :, 0]
        if cut is not None:

            @pl.when(pl.program_id(0) < cut)
            def _():
                scr[:, 1] = ins[1][:, :, 0]

            @pl.when(pl.program_id(0) >= cut)
            def _():
                scr[:, 1] = ins[2][:, :, 0]
        else:
            scr[:, 1] = ins[1][:, :, 0]
        regrouped = scr[...].reshape(BS, T)
        if backward:
            branch = dot(regrouped.T, w_ref[0], 1, 1)
        else:
            branch = dot(regrouped, w_ref[0], 0, 0)
            slab_scr[...] = regrouped.reshape(Q, 2, rows, T)
        out_ref[...] = (base_ref[...].astype(F32) + branch).astype(BF16)
        for send in (True, False):
            which = 1 - core if send else core
            if backward:
                half = left_ref[0, :, which].reshape(Q * rows, T)
                part = dot(half, regrouped, 1, 1)
            else:
                half = slab_scr[:, which].reshape(Q * rows, T)
                part = dot(half, left_ref[...], 1, 0)
            part = (scale * part).astype(BF16).reshape(Q, rows, BS)
            if send:
                low_ref[0], high_ref[0] = part[:, : rows // 2], part[:, rows // 2 :]
            else:
                low_keep[0], high_keep[0] = part[:, : rows // 2], part[:, rows // 2 :]

    cols = spec((T, BS), lambda b, s: (0, first + b))
    piece = jax.ShapeDtypeStruct((count, Q, rows // 2, BS), BF16)
    piece_spec = spec((1, Q, rows // 2, BS), lambda b, s: (b, 0, 0, 0))
    left_spec = spec((1, Q, 2, rows, T), lambda b, s: (first + b, 0, 0, 0, 0)) if backward else cols
    operands = held(*received, weight, base_rows, left)
    more, aliases = [], {}
    if onto is not None:
        operands += held(onto)
        more, aliases = [pl.BlockSpec(memory_space=pl.ANY)], {n_in + 4: 0}
    return pl.pallas_call(
        kernel,
        name="leave_back" if backward else "leave_out",
        grid_spec=pltpu.PrefetchScalarGridSpec(
            num_scalar_prefetch=1,
            grid=(count,),
            in_specs=[
                spec((NT, G, 1, SW, T), lambda b, s, place=place: (0, 0, place(b), 0, 0)) for place in places
            ]
            + [spec((1, BS, BS), lambda b, s: (first + b, 0, 0)), cols, left_spec]
            + more,
            out_specs=[cols] + [piece_spec] * 4,
            scratch_shapes=[
                pltpu.VMEM((NT, N_CHUNK, G, SW, T), BF16),
                pltpu.VMEM((Q, 2, rows, T), BF16),
            ],
        ),
        out_shape=[pltpu.HBM((T, L * BS), BF16)] + [piece] * 4,
        input_output_aliases=aliases,
        compiler_params=params(24),
        cost_estimate=LIGHT,
    )(where, *operands)


def together(*values):
    return lax.optimization_barrier(values)


def regroup(pieces, label):
    with jax.named_scope(label):
        return lax.all_to_all(pieces, "tensor", split_axis=0, concat_axis=0, tiled=True)


def swap(value, bit, label):
    count = lax.axis_size("dp")
    with jax.named_scope(label):
        return lax.ppermute(value, "dp", [(s, s ^ (1 << bit)) for s in range(count)])


def split(which, pairs, sizes):
    lead, count = sizes
    n = len(pairs)

    def kernel(which_ref, *refs):
        ins, outs = refs[: 4 * n], refs[4 * n :]
        for i in range(2 * n):
            a, b = ins[2 * i][...].astype(F32), ins[2 * i + 1][...].astype(F32)
            outs[i][...] = (a + b).astype(BF16)

    in_specs, operands, out_specs, out_shape = [], [], [], []
    for i, (keep, got, first, place) in enumerate(pairs):
        rows, width = keep.shape[2:]
        for stays in (0, 1):

            def index(a, r, which_ref, i=i, first=first, place=place, stays=stays):
                mine = which_ref[i]
                chosen = mine if stays else 1 - mine
                low = r & ((1 << place) - 1)
                return (first + a, ((r >> place) << (place + 1)) | (chosen << place) | low, 0, 0)

            in_specs += [spec((1, 1, rows, width), index)] * 2
            operands += [keep, got]
            out_specs.append(spec((1, 1, rows, width), lambda a, r, w: (a, r, 0, 0)))
            out_shape.append(pltpu.HBM((lead, count // 2, rows, width), BF16))
    outs = pl.pallas_call(
        kernel,
        name="split",
        grid_spec=pltpu.PrefetchScalarGridSpec(
            num_scalar_prefetch=1, grid=(lead, count // 2), in_specs=in_specs, out_specs=out_specs
        ),
        out_shape=out_shape,
        compiler_params=params(16),
        cost_estimate=LIGHT,
    )(which, *held(*operands))
    return [(outs[2 * i], outs[2 * i + 1]) for i in range(n)]


def whole():
    return pl.BlockSpec(memory_space=pltpu.VMEM)


def split_small(which, pairs, lead):
    n = len(pairs)
    operands = []
    for keep, got, _, _ in pairs:
        operands += [keep] + list(got)

    def kernel(which_ref, *refs):
        ins, outs = list(refs[: len(operands)]), refs[len(operands) :]
        for i, (keep, got, first, place) in enumerate(pairs):
            keep_ref, got_refs = ins.pop(0), [ins.pop(0) for _ in got]
            for stays in (0, 1):
                chosen = which_ref[i] if stays else 1 - which_ref[i]
                for r in range(keep.shape[1] // 2):
                    low = r & ((1 << place) - 1)
                    q = ((r >> place) << (place + 1)) + low + chosen * (1 << place)
                    for a in range(lead):
                        start = 0
                        for got_ref, came in zip(got_refs, got):
                            stop = start + came.shape[2]
                            total = keep_ref[first + a, q, start:stop].astype(F32) + got_ref[first + a, q].astype(F32)
                            outs[2 * i + stays][a, r, start:stop] = total.astype(BF16)
                            start = stop

    out_shape = []
    for keep, _, _, _ in pairs:
        out_shape += [jax.ShapeDtypeStruct((lead, keep.shape[1] // 2) + keep.shape[2:], BF16)] * 2
    outs = pl.pallas_call(
        kernel,
        name="small",
        in_specs=[pl.BlockSpec(memory_space=pltpu.SMEM)] + [whole()] * len(operands),
        out_specs=[whole()] * (2 * n),
        out_shape=out_shape,
        compiler_params=params(8),
        cost_estimate=LIGHT,
    )(which, *operands)
    return [(outs[2 * i], outs[2 * i + 1]) for i in range(n)]


def finish(groups):
    flat, shapes = [], []
    for pairs in groups:
        leads, rows = 0, 0
        for pair in pairs:
            halves = pair if isinstance(pair[0], tuple) else (pair,)
            leads += halves[0][0].shape[0]
            rows = sum(keep.shape[2] for keep, _ in halves)
            flat += [array for half in halves for array in half]
        shapes.append((leads, rows, flat[-1].shape[3]))

    def kernel(*refs):
        ins, outs = list(refs[: len(flat)]), refs[len(flat) :]
        for pairs, out in zip(groups, outs):
            start = 0
            for pair in pairs:
                halves = pair if isinstance(pair[0], tuple) else (pair,)
                row, leads = 0, halves[0][0].shape[0]
                for keep, _ in halves:
                    a, b = ins.pop(0), ins.pop(0)
                    rows = keep.shape[2]
                    out[start : start + leads, row : row + rows] = a[:, 0].astype(F32) + b[:, 0].astype(F32)
                    row += rows
                start += leads

    return pl.pallas_call(
        kernel,
        name="finish",
        in_specs=[whole()] * len(flat),
        out_shape=[jax.ShapeDtypeStruct(shape, F32) for shape in shapes],
        compiler_params=params(16),
        cost_estimate=LIGHT,
    )(*flat)


class Halving:
    def __init__(self, streams, label, large, turned=0):
        self.label = label
        self.large = large
        self.bits = bits = (lax.axis_size("dp") // 2).bit_length() - 1
        self.orders = [list(range(bits))[:: -1 if (i + turned) % 2 else 1] for i in range(len(streams))]
        self.held = [list(range(bits)) for _ in streams]
        self.streams = streams

    def add(self, lead):
        index = lax.axis_index("dp")
        pairs, mine = [], []
        self.moving = []
        for (keep, got, first), order, held in zip(self.streams, self.orders, self.held):
            bit = order.pop(0)
            pairs.append((keep, got, first, held.index(bit)))
            held.remove(bit)
            mine.append((index >> (bit + 1)) & 1)
            self.moving.append(bit)
        which = jnp.stack(mine).astype(jnp.int32)
        if self.large and len(self.held[0]) == self.bits - 1:
            pairs = [(keep, got[0], first, place) for keep, got, first, place in pairs]
            self.parts = split(which, pairs, (lead, pairs[0][0].shape[1]))
        else:
            self.parts = split_small(which, pairs, lead)
        return [outgoing for outgoing, _ in self.parts]

    def move(self, outgoing):
        self.streams = [
            (staying, [swap(out, bit + 1, "%s_bit%d" % (self.label, bit))], 0)
            for out, (_, staying), bit in zip(outgoing, self.parts, self.moving)
        ]

    def got(self):
        return [array for _, got, _ in self.streams for array in got]

    def replace(self, arrived):
        arrived = list(arrived)
        self.streams = [
            (keep, [arrived.pop(0) for _ in got], first) for keep, got, first in self.streams
        ]

    def run(self, lead):
        while self.orders[0]:
            self.move(self.add(lead))
        return [(keep, got[0]) for keep, got, _ in self.streams]


def body(tokens, up_first, up_second, down_first, down_second, cotangent):
    T = tokens.shape[0]
    L, BS = up_first.shape[0], up_first.shape[1]
    HB = up_second.shape[2]
    NT = lax.axis_size("tensor")
    n_dp = lax.axis_size("dp")
    scale = (T * n_dp) ** (-0.5)
    sizes = (T, L, BS, NT, L // N_CHUNK, BS // NB, n_dp // 2, HB)
    where = (lax.axis_index("dp") % 2).astype(jnp.int32).reshape(1)

    lead = L // N_CHUNK
    half = L // 2
    cut = max(L // 4, 1)

    def middle_sums(parts, label, before):
        (up_send, up_keep), (down_send, down_keep) = parts
        if before is not None:
            up_send, down_send, *got = together(up_send, down_send, *before.got())
            before.replace(got)
        got_up, got_down = swap(up_send, 0, label + "_core"), swap(down_send, 0, label + "_core")
        return Halving([(up_keep, [got_up], 0), (down_keep, [got_down], 0)], label, True)

    first_0, first_1 = enter(tokens, up_first, cotangent, down_second, sizes)
    in_0 = regroup(first_0, "z1")
    x_turned = turn(tokens, sizes)
    in_0, first_1, x_turned = together(in_0, first_1, x_turned)
    in_1 = regroup(first_1, "z2")
    (both_0,), *parts = middle(where, in_0, up_second, down_first, 0, scale, sizes, True)
    mid_0 = middle_sums(parts, "mid0", None)
    leaving_0 = mid_0.add(lead)
    in_1, both_0, *_ = together(in_1, both_0, *leaving_0)
    both_0 = regroup(both_0, "z3")
    mid_0.move(leaving_0)
    (most_1, rest_1), *parts = middle(where, in_1, up_second, down_first, 1, scale, sizes, False)
    mid_1 = middle_sums(parts, "mid1", mid_0)
    leaving_0 = mid_0.add(lead)
    mid_0.move(leaving_0)
    both_0, most_1, *got = together(both_0, most_1, *mid_0.got())
    mid_0.replace(got)
    most_1 = regroup(most_1, "z4")
    leaving_1 = mid_1.add(lead)
    mid_1.move(leaving_1)
    most_1, rest_1, *_ = together(most_1, rest_1, *leaving_1)
    rest_1 = regroup(rest_1, "z5")
    def edge_sums(halves, label):
        streams = [(keep, [swap(out, 0, label + "_core")], 0) for out, keep in zip(halves[:2], halves[2:])]
        return Halving(streams, label, False)

    grad_tokens, *first = leave(
        where, (both_0, most_1), [lambda b: b] * 2, up_first, cotangent, x_turned, scale, sizes, True, 0, L
    )
    edge_first = edge_sums(first, "first")
    leaving_first = edge_first.add(L)
    leaving_1 = mid_1.add(lead) if mid_1.orders[0] else []
    edge_first.move(leaving_first)
    mid_1.move(leaving_1)
    rest_1, *_ = together(rest_1, *leaving_first, *leaving_1)
    layer_out, *high = leave(
        where,
        (both_0, most_1, rest_1),
        [lambda b: L + b, lambda b: L + jnp.minimum(b, cut - 1), lambda b: jnp.maximum(b - cut, 0)],
        down_second,
        tokens,
        cotangent,
        scale,
        sizes,
        False,
        0,
        L,
        None,
        cut,
    )
    waited = (mid_1,)
    high[0], high[1], *got = together(*high[:2], *[array for sums in waited for array in sums.got()])
    for sums in waited:
        count = len(sums.got())
        sums.replace(got[:count])
        got = got[count:]
    edge_high = edge_sums(high, "high")
    edge_high.move(edge_high.add(L))
    done_0, done_1 = mid_0.run(lead), mid_1.run(lead)
    grad_up_second, grad_down_first = finish([[done_0[0], done_1[0]], [done_0[1], done_1[1]]])
    done_first = edge_first.run(L)
    got = together(*edge_high.got(), grad_up_second, grad_down_first)
    edge_high.replace(got[:-2])
    done_high = edge_high.run(L)
    (grad_up_first,) = finish([[tuple(done_first)]])
    (grad_down_second,) = finish([[tuple(done_high)]])
    return (
        layer_out,
        grad_tokens,
        grad_up_first.reshape(L, -1, BS),
        got[-2].reshape(L, -1, HB),
        got[-1].reshape(L, -1, BS),
        grad_down_second.reshape(L, -1, BS),
    )


def solution(mesh):
    in_specs = (
        P("dp", "tensor"),
        P("tensor", None, None),
        P("tensor", None, None),
        P("tensor", None, None),
        P("tensor", None, None),
        P("dp", "tensor"),
    )
    out_specs = (
        P("dp", "tensor"),
        P("dp", "tensor"),
        P("tensor", "dp", None),
        P("tensor", "dp", None),
        P("tensor", "dp", None),
        P("tensor", "dp", None),
    )
    return jax.shard_map(body, mesh=mesh, in_specs=in_specs, out_specs=out_specs, check_vma=False)
```

```python
import jax
import jax.numpy as jnp
from jax import lax
from jax.experimental import pallas as pl
from jax.experimental.pallas import tpu as pltpu
from jax.sharding import PartitionSpec as P

NB = 16
N_CHUNK = 2

gelu_coeff = 0.7978845608028654
cubic_coeff = 0.044715

BF16 = jnp.bfloat16
F32 = jnp.float32


def gelu_pair(hidden):
    inner_arg = gelu_coeff * (hidden + cubic_coeff * hidden * hidden * hidden)
    tangent = jnp.tanh(inner_arg)
    gelu_value = 0.5 * hidden * (1.0 + tangent)
    gelu_slope = 0.5 * (1.0 + tangent) + 0.5 * hidden * (1.0 - tangent * tangent) * gelu_coeff * (
        1.0 + 3.0 * cubic_coeff * hidden * hidden
    )
    return gelu_value, gelu_slope


def dot(a, b, ca, cb):
    return lax.dot_general(a, b, (((ca,), (cb,)), ((), ())), preferred_element_type=F32)


def params(mebibytes):
    return pltpu.CompilerParams(vmem_limit_bytes=mebibytes * 1024 * 1024)


def held(*values):
    return [pltpu.with_memory_space_constraint(v, pltpu.HBM) for v in values]


def spec(block, index_map):
    return pl.BlockSpec(block, index_map)


LIGHT = pl.CostEstimate(flops=0, transcendentals=0, bytes_accessed=0)


def enter(tokens, up_first, cotangent, down_second, sizes):
    T, L, BS, NT, G, SW, Q, _ = sizes

    def kernel(x_ref, w_ref, g_ref, d_ref, *outs):
        up = dot(x_ref[...], w_ref[0], 1, 0).astype(BF16).T.reshape(NT, L, SW, T)
        back = dot(d_ref[0], g_ref[...], 1, 1).astype(BF16).reshape(NT, L, SW, T)
        for chunk in range(N_CHUNK):
            outs[chunk][:, 0, :, 0] = up[:, chunk * G : (chunk + 1) * G]
            outs[chunk][:, 1, :, 0] = back[:, chunk * G : (chunk + 1) * G]

    cols = spec((T, BS), lambda b: (0, b))
    square = spec((1, BS, BS), lambda b: (b, 0, 0))
    outs = pl.pallas_call(
        kernel,
        name="enter",
        grid=(L,),
        in_specs=[cols, square, cols, square],
        out_specs=[spec((NT, 2, G, 1, SW, T), lambda b: (0, 0, 0, b, 0, 0))] * N_CHUNK,
        out_shape=[pltpu.HBM((NT, 2, G, L, SW, T), BF16)] * N_CHUNK,
        compiler_params=params(56),
        cost_estimate=LIGHT,
    )(*held(tokens, up_first, cotangent, down_second))
    return outs


def turn(tokens, sizes):
    T, L, BS, _, _, _, Q, _ = sizes
    rows = BS // (2 * Q)

    def kernel(x_ref, out_ref):
        out_ref[0] = x_ref[...].T.reshape(Q, 2, rows, T)

    return pl.pallas_call(
        kernel,
        name="turn",
        grid=(L,),
        in_specs=[spec((T, BS), lambda b: (0, b))],
        out_specs=spec((1, Q, 2, rows, T), lambda b: (b, 0, 0, 0, 0)),
        out_shape=pltpu.HBM((L, Q, 2, rows, T), BF16),
        compiler_params=params(56),
        cost_estimate=LIGHT,
    )(*held(tokens))


def middle(where, received, up_second, down_first, chunk, scale, sizes, joint):
    T, L, BS, NT, G, SW, Q, HB = sizes
    rows_up, rows_down = BS // (2 * Q), HB // (2 * Q)
    cut = max(L // 4, 1)
    tile = min(512, HB)

    def kernel(where_ref, *refs):
        in_ref, up_ref, down_ref = refs[:3]
        up_send, up_keep, down_send, down_keep, rs_scr, act_scr, at_scr, gp_scr = refs[-8:]
        core = where_ref[0]
        regrouped = in_ref[:, 0, 0].reshape(BS, T)
        rs_scr[...] = regrouped.reshape(Q, 2, rows_up, T)
        turned = regrouped.T
        grad_mid = in_ref[:, 1, 0].reshape(BS, T).T
        for start in range(0, HB, tile):
            pre = dot(turned, up_ref[0, :, start : start + tile], 1, 0)
            value, slope = gelu_pair(pre)
            value = value.astype(BF16)
            act_scr[:, start : start + tile] = value
            at_scr[start : start + tile] = value.T
            grad_act = dot(grad_mid, down_ref[0, start : start + tile], 1, 1)
            gp_scr[:, start : start + tile] = (grad_act * slope).astype(BF16)
        activated = act_scr[...]
        grad_pre = gp_scr[...]
        down = dot(activated, down_ref[0], 1, 0).astype(BF16).T.reshape(NT, L, SW, T)
        back = dot(grad_pre, up_ref[0], 1, 1).astype(BF16).T.reshape(NT, L, SW, T)
        if joint:
            refs[3][:, 0, :L] = back
            refs[3][:, 0, L:] = down
        else:
            refs[3][:, 0, :L] = back
            refs[3][:, 0, L:] = down[:, :cut]
            refs[4][:, 0] = down[:, cut:]
        for send, ref in ((True, up_send), (False, up_keep)):
            half = rs_scr[:, 1 - core if send else core].reshape(Q * rows_up, T)
            part = scale * dot(half, grad_pre, 1, 0)
            ref[0] = part.astype(BF16).reshape(Q, rows_up, HB)
        for send, ref in ((True, down_send), (False, down_keep)):
            for q in range(Q):
                first = (2 * q + (1 - core if send else core)) * rows_down
                half = at_scr[pl.ds(pl.multiple_of(first, rows_down), rows_down)]
                ref[0, q] = (scale * dot(half, grad_mid, 1, 0)).astype(BF16)

    base = chunk * G
    widths = [2 * L] if joint else [L + cut, L - cut]
    pieces = [pltpu.HBM((NT, G, w, SW, T), BF16) for w in widths]
    piece_specs = [spec((NT, 1, w, SW, T), lambda g, s: (0, g, 0, 0, 0)) for w in widths]
    up_part = pltpu.HBM((G, Q, rows_up, HB), BF16)
    down_part = pltpu.HBM((G, Q, rows_down, BS), BF16)
    outs = pl.pallas_call(
        kernel,
        name="middle",
        grid_spec=pltpu.PrefetchScalarGridSpec(
            num_scalar_prefetch=1,
            grid=(G,),
            in_specs=[
                spec((NT, 2, 1, L, SW, T), lambda g, s: (0, 0, g, 0, 0, 0)),
                spec((1, BS, HB), lambda g, s: (base + g, 0, 0)),
                spec((1, HB, BS), lambda g, s: (base + g, 0, 0)),
            ],
            out_specs=piece_specs
            + [spec((1, Q, rows_up, HB), lambda g, s: (g, 0, 0, 0))] * 2
            + [spec((1, Q, rows_down, BS), lambda g, s: (g, 0, 0, 0))] * 2,
            scratch_shapes=[
                pltpu.VMEM((Q, 2, rows_up, T), BF16),
                pltpu.VMEM((T, HB), BF16),
                pltpu.VMEM((HB, T), BF16),
                pltpu.VMEM((T, HB), BF16),
            ],
        ),
        out_shape=pieces + [up_part] * 2 + [down_part] * 2,
        compiler_params=params(32),
        cost_estimate=LIGHT,
    )(where, *held(received, up_second, down_first))
    return outs[:-4], outs[-4:-2], outs[-2:]


def leave(where, received, places, weight, base_rows, left, scale, sizes, backward, first, count, onto=None, cut=None):
    T, L, BS, NT, G, SW, Q, _ = sizes
    rows = BS // (2 * Q)
    n_in = len(places)

    def kernel(where_ref, *refs):
        ins, (w_ref, base_ref, left_ref) = refs[:n_in], refs[n_in : n_in + 3]
        out_ref, low_ref, high_ref, low_keep, high_keep, scr, slab_scr = refs[-7:]
        core = where_ref[0]
        scr[:, 0] = ins[0][:, :, 0]
        if cut is not None:

            @pl.when(pl.program_id(0) < cut)
            def _():
                scr[:, 1] = ins[1][:, :, 0]

            @pl.when(pl.program_id(0) >= cut)
            def _():
                scr[:, 1] = ins[2][:, :, 0]
        else:
            scr[:, 1] = ins[1][:, :, 0]
        regrouped = scr[...].reshape(BS, T)
        if backward:
            branch = dot(regrouped.T, w_ref[0], 1, 1)
        else:
            branch = dot(regrouped, w_ref[0], 0, 0)
            slab_scr[...] = regrouped.reshape(Q, 2, rows, T)
        out_ref[...] = (base_ref[...].astype(F32) + branch).astype(BF16)
        for send in (True, False):
            which = 1 - core if send else core
            if backward:
                half = left_ref[0, :, which].reshape(Q * rows, T)
                part = dot(half, regrouped, 1, 1)
            else:
                half = slab_scr[:, which].reshape(Q * rows, T)
                part = dot(half, left_ref[...], 1, 0)
            part = (scale * part).astype(BF16).reshape(Q, rows, BS)
            if send:
                low_ref[0], high_ref[0] = part[:, : rows // 2], part[:, rows // 2 :]
            else:
                low_keep[0], high_keep[0] = part[:, : rows // 2], part[:, rows // 2 :]

    cols = spec((T, BS), lambda b, s: (0, first + b))
    piece = jax.ShapeDtypeStruct((count, Q, rows // 2, BS), BF16)
    piece_spec = spec((1, Q, rows // 2, BS), lambda b, s: (b, 0, 0, 0))
    left_spec = spec((1, Q, 2, rows, T), lambda b, s: (first + b, 0, 0, 0, 0)) if backward else cols
    operands = held(*received, weight, base_rows, left)
    more, aliases = [], {}
    if onto is not None:
        operands += held(onto)
        more, aliases = [pl.BlockSpec(memory_space=pl.ANY)], {n_in + 4: 0}
    return pl.pallas_call(
        kernel,
        name="leave_back" if backward else "leave_out",
        grid_spec=pltpu.PrefetchScalarGridSpec(
            num_scalar_prefetch=1,
            grid=(count,),
            in_specs=[
                spec((NT, G, 1, SW, T), lambda b, s, place=place: (0, 0, place(b), 0, 0)) for place in places
            ]
            + [spec((1, BS, BS), lambda b, s: (first + b, 0, 0)), cols, left_spec]
            + more,
            out_specs=[cols] + [piece_spec] * 4,
            scratch_shapes=[
                pltpu.VMEM((NT, N_CHUNK, G, SW, T), BF16),
                pltpu.VMEM((Q, 2, rows, T), BF16),
            ],
        ),
        out_shape=[pltpu.HBM((T, L * BS), BF16)] + [piece] * 4,
        input_output_aliases=aliases,
        compiler_params=params(24),
        cost_estimate=LIGHT,
    )(where, *operands)


def together(*values):
    return lax.optimization_barrier(values)


def regroup(pieces, label):
    with jax.named_scope(label):
        return lax.all_to_all(pieces, "tensor", split_axis=0, concat_axis=0, tiled=True)


def swap(value, bit, label):
    count = lax.axis_size("dp")
    with jax.named_scope(label):
        return lax.ppermute(value, "dp", [(s, s ^ (1 << bit)) for s in range(count)])


def split(which, pairs, sizes):
    lead, count = sizes
    n = len(pairs)

    def kernel(which_ref, *refs):
        ins, outs = refs[: 4 * n], refs[4 * n :]
        for i in range(2 * n):
            a, b = ins[2 * i][...].astype(F32), ins[2 * i + 1][...].astype(F32)
            outs[i][...] = (a + b).astype(BF16)

    in_specs, operands, out_specs, out_shape = [], [], [], []
    for i, (keep, got, first, place) in enumerate(pairs):
        rows, width = keep.shape[2:]
        for stays in (0, 1):

            def index(a, r, which_ref, i=i, first=first, place=place, stays=stays):
                mine = which_ref[i]
                chosen = mine if stays else 1 - mine
                low = r & ((1 << place) - 1)
                return (first + a, ((r >> place) << (place + 1)) | (chosen << place) | low, 0, 0)

            in_specs += [spec((1, 1, rows, width), index)] * 2
            operands += [keep, got]
            out_specs.append(spec((1, 1, rows, width), lambda a, r, w: (a, r, 0, 0)))
            out_shape.append(pltpu.HBM((lead, count // 2, rows, width), BF16))
    outs = pl.pallas_call(
        kernel,
        name="split",
        grid_spec=pltpu.PrefetchScalarGridSpec(
            num_scalar_prefetch=1, grid=(lead, count // 2), in_specs=in_specs, out_specs=out_specs
        ),
        out_shape=out_shape,
        compiler_params=params(16),
        cost_estimate=LIGHT,
    )(which, *held(*operands))
    return [(outs[2 * i], outs[2 * i + 1]) for i in range(n)]


def whole():
    return pl.BlockSpec(memory_space=pltpu.VMEM)


def split_small(which, pairs, lead):
    n = len(pairs)
    operands = []
    for keep, got, _, _ in pairs:
        operands += [keep] + list(got)

    def kernel(which_ref, *refs):
        ins, outs = list(refs[: len(operands)]), refs[len(operands) :]
        for i, (keep, got, first, place) in enumerate(pairs):
            keep_ref, got_refs = ins.pop(0), [ins.pop(0) for _ in got]
            for stays in (0, 1):
                chosen = which_ref[i] if stays else 1 - which_ref[i]
                for r in range(keep.shape[1] // 2):
                    low = r & ((1 << place) - 1)
                    q = ((r >> place) << (place + 1)) + low + chosen * (1 << place)
                    for a in range(lead):
                        start = 0
                        for got_ref, came in zip(got_refs, got):
                            stop = start + came.shape[2]
                            total = keep_ref[first + a, q, start:stop].astype(F32) + got_ref[first + a, q].astype(F32)
                            outs[2 * i + stays][a, r, start:stop] = total.astype(BF16)
                            start = stop

    out_shape = []
    for keep, _, _, _ in pairs:
        out_shape += [jax.ShapeDtypeStruct((lead, keep.shape[1] // 2) + keep.shape[2:], BF16)] * 2
    outs = pl.pallas_call(
        kernel,
        name="small",
        in_specs=[pl.BlockSpec(memory_space=pltpu.SMEM)] + [whole()] * len(operands),
        out_specs=[whole()] * (2 * n),
        out_shape=out_shape,
        compiler_params=params(8),
        cost_estimate=LIGHT,
    )(which, *operands)
    return [(outs[2 * i], outs[2 * i + 1]) for i in range(n)]


def finish(groups):
    flat, shapes = [], []
    for pairs in groups:
        leads, rows = 0, 0
        for pair in pairs:
            halves = pair if isinstance(pair[0], tuple) else (pair,)
            leads += halves[0][0].shape[0]
            rows = sum(keep.shape[2] for keep, _ in halves)
            flat += [array for half in halves for array in half]
        shapes.append((leads, rows, flat[-1].shape[3]))

    def kernel(*refs):
        ins, outs = list(refs[: len(flat)]), refs[len(flat) :]
        for pairs, out in zip(groups, outs):
            start = 0
            for pair in pairs:
                halves = pair if isinstance(pair[0], tuple) else (pair,)
                row, leads = 0, halves[0][0].shape[0]
                for keep, _ in halves:
                    a, b = ins.pop(0), ins.pop(0)
                    rows = keep.shape[2]
                    out[start : start + leads, row : row + rows] = a[:, 0].astype(F32) + b[:, 0].astype(F32)
                    row += rows
                start += leads

    return pl.pallas_call(
        kernel,
        name="finish",
        in_specs=[whole()] * len(flat),
        out_shape=[jax.ShapeDtypeStruct(shape, F32) for shape in shapes],
        compiler_params=params(16),
        cost_estimate=LIGHT,
    )(*flat)


class Halving:
    def __init__(self, streams, label, large, turned=0):
        self.label = label
        self.large = large
        self.bits = bits = (lax.axis_size("dp") // 2).bit_length() - 1
        self.orders = [list(range(bits))[:: -1 if (i + turned) % 2 else 1] for i in range(len(streams))]
        self.held = [list(range(bits)) for _ in streams]
        self.streams = streams

    def add(self, lead):
        index = lax.axis_index("dp")
        pairs, mine = [], []
        self.moving = []
        for (keep, got, first), order, held in zip(self.streams, self.orders, self.held):
            bit = order.pop(0)
            pairs.append((keep, got, first, held.index(bit)))
            held.remove(bit)
            mine.append((index >> (bit + 1)) & 1)
            self.moving.append(bit)
        which = jnp.stack(mine).astype(jnp.int32)
        if self.large and len(self.held[0]) == self.bits - 1:
            pairs = [(keep, got[0], first, place) for keep, got, first, place in pairs]
            self.parts = split(which, pairs, (lead, pairs[0][0].shape[1]))
        else:
            self.parts = split_small(which, pairs, lead)
        return [outgoing for outgoing, _ in self.parts]

    def move(self, outgoing):
        self.streams = [
            (staying, [swap(out, bit + 1, "%s_bit%d" % (self.label, bit))], 0)
            for out, (_, staying), bit in zip(outgoing, self.parts, self.moving)
        ]

    def got(self):
        return [array for _, got, _ in self.streams for array in got]

    def replace(self, arrived):
        arrived = list(arrived)
        self.streams = [
            (keep, [arrived.pop(0) for _ in got], first) for keep, got, first in self.streams
        ]

    def run(self, lead):
        while self.orders[0]:
            self.move(self.add(lead))
        return [(keep, got[0]) for keep, got, _ in self.streams]


def body(tokens, up_first, up_second, down_first, down_second, cotangent):
    T = tokens.shape[0]
    L, BS = up_first.shape[0], up_first.shape[1]
    HB = up_second.shape[2]
    NT = lax.axis_size("tensor")
    n_dp = lax.axis_size("dp")
    scale = (T * n_dp) ** (-0.5)
    sizes = (T, L, BS, NT, L // N_CHUNK, BS // NB, n_dp // 2, HB)
    where = (lax.axis_index("dp") % 2).astype(jnp.int32).reshape(1)

    lead = L // N_CHUNK
    half = L // 2
    cut = max(L // 4, 1)

    def middle_sums(parts, label, before):
        (up_send, up_keep), (down_send, down_keep) = parts
        if before is not None:
            up_send, down_send, *got = together(up_send, down_send, *before.got())
            before.replace(got)
        got_up, got_down = swap(up_send, 0, label + "_core"), swap(down_send, 0, label + "_core")
        return Halving([(up_keep, [got_up], 0), (down_keep, [got_down], 0)], label, True)

    first_0, first_1 = enter(tokens, up_first, cotangent, down_second, sizes)
    in_0 = regroup(first_0, "z1")
    x_turned = turn(tokens, sizes)
    in_0, first_1, x_turned = together(in_0, first_1, x_turned)
    in_1 = regroup(first_1, "z2")
    (both_0,), *parts = middle(where, in_0, up_second, down_first, 0, scale, sizes, True)
    mid_0 = middle_sums(parts, "mid0", None)
    leaving_0 = mid_0.add(lead)
    in_1, both_0, *_ = together(in_1, both_0, *leaving_0)
    both_0 = regroup(both_0, "z3")
    mid_0.move(leaving_0)
    (most_1, rest_1), *parts = middle(where, in_1, up_second, down_first, 1, scale, sizes, False)
    mid_1 = middle_sums(parts, "mid1", mid_0)
    leaving_0 = mid_0.add(lead)
    mid_0.move(leaving_0)
    both_0, most_1, *got = together(both_0, most_1, *mid_0.got())
    mid_0.replace(got)
    most_1 = regroup(most_1, "z4")
    leaving_1 = mid_1.add(lead)
    mid_1.move(leaving_1)
    most_1, rest_1, *_ = together(most_1, rest_1, *leaving_1)
    rest_1 = regroup(rest_1, "z5")
    def edge_sums(halves, label):
        streams = [(keep, [swap(out, 0, label + "_core")], 0) for out, keep in zip(halves[:2], halves[2:])]
        return Halving(streams, label, False)

    grad_tokens, *first = leave(
        where, (both_0, most_1), [lambda b: b] * 2, up_first, cotangent, x_turned, scale, sizes, True, 0, L
    )
    edge_first = edge_sums(first, "first")
    leaving_first = edge_first.add(L)
    leaving_1 = mid_1.add(lead) if mid_1.orders[0] else []
    edge_first.move(leaving_first)
    mid_1.move(leaving_1)
    rest_1, *_ = together(rest_1, *leaving_first, *leaving_1)
    layer_out, *high = leave(
        where,
        (both_0, most_1, rest_1),
        [lambda b: L + b, lambda b: L + jnp.minimum(b, cut - 1), lambda b: jnp.maximum(b - cut, 0)],
        down_second,
        tokens,
        cotangent,
        scale,
        sizes,
        False,
        0,
        L,
        None,
        cut,
    )
    waited = (edge_first, mid_1)
    high[0], high[1], *got = together(*high[:2], *[array for sums in waited for array in sums.got()])
    for sums in waited:
        count = len(sums.got())
        sums.replace(got[:count])
        got = got[count:]
    edge_high = edge_sums(high, "high")
    edge_high.move(edge_high.add(L))
    done_0, done_1 = mid_0.run(lead), mid_1.run(lead)
    grad_up_second, grad_down_first = finish([[done_0[0], done_1[0]], [done_0[1], done_1[1]]])
    done_first = edge_first.run(L)
    got = together(*edge_high.got(), grad_up_second, grad_down_first)
    edge_high.replace(got[:-2])
    done_high = edge_high.run(L)
    (grad_up_first,) = finish([[tuple(done_first)]])
    (grad_down_second,) = finish([[tuple(done_high)]])
    return (
        layer_out,
        grad_tokens,
        grad_up_first.reshape(L, -1, BS),
        got[-2].reshape(L, -1, HB),
        got[-1].reshape(L, -1, BS),
        grad_down_second.reshape(L, -1, BS),
    )


def solution(mesh):
    in_specs = (
        P("dp", "tensor"),
        P("tensor", None, None),
        P("tensor", None, None),
        P("tensor", None, None),
        P("tensor", None, None),
        P("dp", "tensor"),
    )
    out_specs = (
        P("dp", "tensor"),
        P("dp", "tensor"),
        P("tensor", "dp", None),
        P("tensor", "dp", None),
        P("tensor", "dp", None),
        P("tensor", "dp", None),
    )
    return jax.shard_map(body, mesh=mesh, in_specs=in_specs, out_specs=out_specs, check_vma=False)
```
